32 devices in a mesh: rep: 4 (over x, core), shard: 8 (over z, y).
Axes of the slice: x: 2, y: 2, z: 4, core: 2. Of those that a mesh axis runs over, the one named last changes fastest.
Arguments:
- inputs: bfloat16 [8, 1024, 2048], P('rep', 'shard'), may hold values from -6 to 6
- out_cotangent: bfloat16 [8, 1024, 2048], P('rep', 'shard'), may hold values from -6 to 6
- slot_length: int32 [8], P('rep'), may hold values from 0 to 1024, as said below
- mixer_norm: bfloat16 [2048], P('shard'), may hold values from 0.5 to 1.5
- mixer_in: bfloat16 [2048, 8192], P('shard'), may hold values from -0.125 to 0.125
- gate_weight: bfloat16 [2048, 4096], P('shard'), may hold values from -0.125 to 0.125
- alpha_beta: bfloat16 [2048, 32], P('shard'), may hold values from -0.125 to 0.125
- conv_taps: bfloat16 [4, 8192], P(None, 'shard'), may hold values from -3 to 3
- decay_log: float32 [16], replicated, may hold values from -6 to -1
- decay_bias: float32 [16], replicated, may hold values from -2 to 1
- head_norm: bfloat16 [256], P('shard'), may hold values from 0.5 to 1.5
- mixer_out: bfloat16 [4096, 2048], P('shard'), may hold values from -0.09375 to 0.09375
- feed_norm: bfloat16 [2048], P('shard'), may hold values from 0.5 to 1.5
- gate_up: bfloat16 [2048, 11264], P('shard'), may hold values from -0.125 to 0.125
- down_weight: bfloat16 [5632, 2048], P('shard'), may hold values from -0.078125 to 0.078125
Outputs:
- layer_out: bfloat16 [8, 1024, 2048], P('rep', 'shard')
- input_grad: bfloat16 [8, 1024, 2048], P('rep', 'shard')
- grad_mixer_norm: float32 [2048], P('shard')
- grad_mixer_in: float32 [2048, 8192], P('shard')
- grad_gate_weight: float32 [2048, 4096], P('shard')
- grad_alpha_beta: float32 [2048, 32], P('shard')
- grad_conv_taps: float32 [4, 8192], P(None, 'shard')
- grad_decay_log: float32 [16], replicated
- grad_decay_bias: float32 [16], replicated
- grad_head_norm: float32 [256], P('shard')
- grad_mixer_out: float32 [4096, 2048], P('shard')
- grad_feed_norm: float32 [2048], P('shard')
- grad_gate_up: float32 [2048, 11264], P('shard')
- grad_down_weight: float32 [5632, 2048], P('shard')
The draws below stay inside these ranges and needn't reach their ends.
Inputs may be any that keep to these rules, and one draw needn't show every extreme that they name: `slot_length`: a slot's live positions, 0 where no sequence is assigned to it; in every draw some slot holds a whole sequence of 1024 positions and some slot holds none.
All inputs are finite; a program needn't handle non-finite values.
Results may differ from the reference program's by a relative error of at most 0.022.
Values may be sent and summed in bfloat16 or wider, within the bound.
No kernel may reach another device: no remote copies, remote signals or barrier semaphores. Data moves between devices by JAX's collectives and lax.ppermute only.
A program may use at most 640 MiB of HBM per device.

```python
import jax
import jax.numpy as jnp
from jax import lax

D = 2048
HEADS = 16
DK = 128
DV = 256
FF = 5632
CONV = 4
SPAN = 64
LENGTH = 1024
SLOTS = 8


def draw_slot_length(key, part):
    first, second = jax.random.split(key)
    lengths = jax.random.randint(first, (SLOTS,), LENGTH // 8, LENGTH + 1)
    order = jax.random.permutation(second, SLOTS)
    lengths = jnp.where(order == 0, LENGTH, lengths)
    lengths = jnp.where(order == 1, 0, lengths)
    return lengths.astype(jnp.int32)


def shard_levels(key, shape, shards, low, top_value):
    loudness, own = 1.0, jax.random.fold_in(key, 6)
    for dim, blocks in shards:
        steps = jnp.exp(jax.random.uniform(jax.random.fold_in(own, dim), (blocks,), jnp.float32, low / len(shards), top_value / len(shards)))
        loudness = loudness * jnp.repeat(steps, shape[dim] // blocks).reshape([-1 if axis == dim else 1 for axis in range(len(shape))])
    return loudness


def bell_draw(key, shape, scale, bound, cuts=(), held_as=jnp.bfloat16):
    level = shard_levels(key, shape, cuts, -0.22, 0.18) if cuts else 1.0
    drawn = jax.random.normal(key, shape, jnp.float32) * scale * level
    return jnp.minimum(jnp.maximum(drawn, -bound), bound).astype(held_as)


def setup_inputs(seed: int = 0) -> dict:
    key_of = jax.random.split(jax.random.key(seed), 16)
    inputs = bell_draw(key_of[0], (SLOTS, LENGTH, D), 1.0, 6.0, ((0, 4), (1, 8)))
    out_cotangent = bell_draw(key_of[1], (SLOTS, LENGTH, D), 1.0, 6.0, ((0, 4), (1, 8)))
    slot_length = draw_slot_length(jax.random.fold_in(key_of[15], 71), 0)
    mixer_norm = jnp.clip(1.0 + 0.1 * jax.random.normal(key_of[3], (D,), jnp.float32), 0.5, 1.5).astype(jnp.bfloat16)
    mixer_in = bell_draw(key_of[4], (D, 2 * HEADS * DK + HEADS * DV), D ** -0.5, 0.125, ((0, 8),))
    gate_weight = bell_draw(key_of[5], (D, HEADS * DV), D ** -0.5, 0.125, ((0, 8),))
    alpha_beta = bell_draw(key_of[6], (D, 2 * HEADS), D ** -0.5, 0.125, ((0, 8),))
    conv_taps = bell_draw(key_of[7], (CONV, 2 * HEADS * DK + HEADS * DV), CONV ** -0.5, 3.0, ((1, 8),))
    decay_log = jnp.clip(jax.random.uniform(key_of[8], (HEADS,), jnp.float32, -6.0, -1.0), -6.0, -1.0)
    decay_bias = jnp.clip(jax.random.uniform(key_of[9], (HEADS,), jnp.float32, -2.0, 1.0), -2.0, 1.0)
    head_norm = jnp.clip(1.0 + 0.1 * jax.random.normal(key_of[10], (DV,), jnp.float32), 0.5, 1.5).astype(jnp.bfloat16)
    mixer_out = bell_draw(key_of[11], (HEADS * DV, D), (HEADS * DV) ** -0.5, 0.09375, ((0, 8),))
    feed_norm = jnp.clip(1.0 + 0.1 * jax.random.normal(key_of[12], (D,), jnp.float32), 0.5, 1.5).astype(jnp.bfloat16)
    gate_up = bell_draw(key_of[13], (D, 2 * FF), D ** -0.5, 0.125, ((0, 8),))
    down_weight = bell_draw(key_of[14], (FF, D), FF ** -0.5, 0.078125, ((0, 8),))
    return {"inputs": inputs, "out_cotangent": out_cotangent, "slot_length": slot_length, "mixer_norm": mixer_norm, "mixer_in": mixer_in, "gate_weight": gate_weight, "alpha_beta": alpha_beta, "conv_taps": conv_taps, "decay_log": decay_log, "decay_bias": decay_bias, "head_norm": head_norm, "mixer_out": mixer_out, "feed_norm": feed_norm, "gate_up": gate_up, "down_weight": down_weight}


HIGH = lax.Precision.HIGHEST
EPS = 1e-06

@jax.custom_vjp
def low(v):
    return lax.optimization_barrier(v.astype(jnp.bfloat16)).astype(jnp.float32)

@jax.custom_vjp
def low_back(v):
    return v

def low_keep(v):
    return (low(v), None)

def low_pass(kept, grad):
    return (grad,)

def back_keep(v):
    return (v, None)

def back_low(kept, grad):
    return (low(grad),)
low.defvjp(low_keep, low_pass)
low_back.defvjp(back_keep, back_low)

def matmul(left, right):
    return jnp.dot(left.astype(jnp.float32), right.astype(jnp.float32), precision=HIGH, preferred_element_type=jnp.float32)

def rms_scale(values, gain):
    return values * lax.rsqrt(lax.optimization_barrier(jnp.mean(values * values, axis=-1, keepdims=True)) + EPS) * gain

def prep_mixer(extended, gate_logits, conv_taps, decay_log, decay_bias):
    count, length = (gate_logits.shape[0], gate_logits.shape[1])
    conv_sum = conv_taps[0] * extended[:, 0:length, :]
    for place in range(1, CONV):
        conv_sum = conv_sum + conv_taps[place] * extended[:, place:place + length, :]
    activated = jax.nn.silu(conv_sum)
    key_width = HEADS * DK
    query_vec = activated[..., :key_width].reshape(count, length, HEADS, DK)
    key_vec = activated[..., key_width:2 * key_width].reshape(count, length, HEADS, DK)
    value_vec = activated[..., 2 * key_width:].reshape(count, length, HEADS, DV)
    query_vec = query_vec * lax.rsqrt(lax.optimization_barrier(jnp.sum(query_vec * query_vec, axis=-1, keepdims=True)) + EPS) * DK ** (-0.5)
    key_vec = key_vec * lax.rsqrt(lax.optimization_barrier(jnp.sum(key_vec * key_vec, axis=-1, keepdims=True)) + EPS)
    gate_beta = jax.nn.sigmoid(gate_logits[..., :HEADS])
    log_decay = -jnp.exp(decay_log) * jax.nn.softplus(gate_logits[..., HEADS:] + decay_bias)
    return (query_vec, key_vec, value_vec, gate_beta, log_decay)

def span_setup(key_vec, gate_beta, log_decay):
    size = log_decay.shape[1]
    cumul = jnp.swapaxes(jnp.cumsum(log_decay, axis=1), 1, 2)
    row_ids = lax.broadcasted_iota(jnp.int32, (size, size), 0)
    col_ids = lax.broadcasted_iota(jnp.int32, (size, size), 1)
    lower = row_ids >= col_ids
    strict = row_ids > col_ids
    spread = cumul[..., :, None] - cumul[..., None, :]
    decay_mat = jnp.where(lower, jnp.exp(jnp.where(lower, spread, 0.0)), 0.0)
    key_heads = jnp.swapaxes(key_vec, 1, 2)
    beta_heads = jnp.swapaxes(gate_beta, 1, 2)
    intersection = jnp.einsum('bhtd,bhsd->bhts', key_heads, key_heads, precision=HIGH)
    system = jnp.eye(size, dtype=jnp.float32) + jnp.where(strict, beta_heads[..., :, None] * decay_mat * intersection, 0.0)
    growth = jnp.exp(cumul)
    tail = jnp.exp(cumul[..., -1:] - cumul)
    return (system, growth, tail, key_heads, beta_heads, decay_mat)

def mix_span(state, pieces):
    query_vec, key_vec, value_vec, gate_beta, log_decay = pieces
    system, growth, tail, key_heads, beta_heads, decay_mat = span_setup(key_vec, gate_beta, log_decay)
    query_heads = jnp.swapaxes(query_vec, 1, 2)
    value_heads = jnp.swapaxes(value_vec, 1, 2)
    right = jnp.concatenate([beta_heads[..., None] * value_heads, (beta_heads * growth)[..., None] * key_heads], axis=-1)
    solved = jax.scipy.linalg.solve_triangular(system, right, lower=True, unit_diagonal=True)
    pseudo = solved[..., :DV] - jnp.einsum('bhck,bhkv->bhcv', solved[..., DV:], state, precision=HIGH)
    scores = jnp.einsum('bhtd,bhsd->bhts', query_heads, key_heads, precision=HIGH) * decay_mat
    output = growth[..., None] * jnp.einsum('bhck,bhkv->bhcv', query_heads, state, precision=HIGH)
    output = output + jnp.einsum('bhts,bhsv->bhtv', scores, pseudo, precision=HIGH)
    carried = growth[..., -1][..., None, None] * state
    carried = carried + jnp.einsum('bhck,bhcv->bhkv', key_heads * tail[..., None], pseudo, precision=HIGH)
    return (carried, jnp.swapaxes(output, 1, 2))

def by_spans(item):
    count, length = (item.shape[0], item.shape[1])
    return jnp.moveaxis(item.reshape((count, length // SPAN, SPAN) + item.shape[2:]), 1, 0)

def segment(query_vec, key_vec, value_vec, gate_beta, log_decay, start):
    count, length = (log_decay.shape[0], log_decay.shape[1])
    pieces = tuple((by_spans(item) for item in (query_vec, key_vec, value_vec, gate_beta, log_decay)))
    carried, outputs = lax.scan(jax.checkpoint(mix_span), start, pieces)
    return (jnp.moveaxis(outputs, 0, 1).reshape(count, length, HEADS, DV), carried)

def out_gate(mixed, gate_pre, head_norm):
    normed = mixed * lax.rsqrt(lax.optimization_barrier(jnp.mean(mixed * mixed, axis=-1, keepdims=True)) + EPS) * head_norm
    count, length = (mixed.shape[0], mixed.shape[1])
    return normed.reshape(count * length, HEADS * DV) * jax.nn.silu(gate_pre)

def swiglu(gate_up_pre):
    return jax.nn.silu(gate_up_pre[:, :FF]) * gate_up_pre[:, FF:]

def layer(params, block_in):
    mixer_norm, mixer_in, gate_weight, alpha_beta, conv_taps, decay_log, decay_bias, head_norm, mixer_out, feed_norm, gate_up, down_weight = params
    count, length, width = block_in.shape
    flat = block_in.reshape(count * length, width)
    normed = low(rms_scale(flat, mixer_norm))
    projected = low_back(low(matmul(normed, mixer_in)))
    gate_pre = low_back(matmul(normed, gate_weight))
    gate_logits = low_back(matmul(normed, alpha_beta))
    proj_seq = projected.reshape(count, length, -1)
    extended = jnp.concatenate([jnp.zeros((count, CONV - 1, proj_seq.shape[2]), jnp.float32), proj_seq], axis=1)
    query_vec, key_vec, value_vec, gate_beta, log_decay = prep_mixer(extended, gate_logits.reshape(count, length, -1), conv_taps, decay_log, decay_bias)
    start = jnp.zeros((count, HEADS, DK, DV), jnp.float32)
    mixed, carried = segment(query_vec, key_vec, value_vec, gate_beta, log_decay, start)
    head_out = low(out_gate(mixed, gate_pre, head_norm))
    resid = flat + low_back(matmul(head_out, mixer_out))
    feed_in = low(rms_scale(resid, feed_norm))
    gate_up_pre = low_back(matmul(feed_in, gate_up))
    hidden = low(swiglu(gate_up_pre))
    result = resid + low_back(matmul(hidden, down_weight))
    return result.reshape(count, length, width)

def reference(inputs, out_cotangent, slot_length, mixer_norm, mixer_in, gate_weight, alpha_beta, conv_taps, decay_log, decay_bias, head_norm, mixer_out, feed_norm, gate_up, down_weight):
    params = tuple((item.astype(jnp.float32) for item in (mixer_norm, mixer_in, gate_weight, alpha_beta, conv_taps, decay_log, decay_bias, head_norm, mixer_out, feed_norm, gate_up, down_weight)))
    positions = jnp.arange(LENGTH, dtype=jnp.int32)
    live = (positions[None, :] < slot_length[:, None]).astype(jnp.float32)
    cotangent = out_cotangent.astype(jnp.float32) * live[..., None]
    blocks = SLOTS // 4
    block_inputs = inputs.astype(jnp.float32).reshape(blocks, 4, LENGTH, D)
    block_cots = cotangent.reshape(blocks, 4, LENGTH, D)
    zero_grads = jax.tree.map(jnp.zeros_like, params)

    def step(accum, item):
        block_in, block_cot = item
        result, pull = jax.vjp(layer, params, block_in)
        grad_params, grad_in = pull(block_cot)
        accum = jax.tree.map(lambda left, right: left + right, accum, grad_params)
        return (accum, (result.astype(jnp.bfloat16), grad_in.astype(jnp.bfloat16)))
    accum, (results, grads_in) = lax.scan(step, zero_grads, (block_inputs, block_cots))
    return (results.reshape(SLOTS, LENGTH, D), grads_in.reshape(SLOTS, LENGTH, D), accum[0], accum[1], accum[2], accum[3], accum[4], accum[5], accum[6], accum[7], accum[8], accum[9], accum[10], accum[11])
```

```python
import functools
import jax
import jax.numpy as jnp
from jax import lax
from jax.experimental import pallas as pl
from jax.experimental.pallas import tpu as pltpu
from jax.sharding import PartitionSpec as P

DK = 128
DV = 256
CONV = 4
SPAN = 64
EPS = 1e-06
F32 = jnp.float32
BF16 = jnp.bfloat16
HIGH = lax.Precision.HIGHEST


def dot(left, right, dims, precision=None):
    return lax.dot_general(
        left, right, ((dims[0], dims[1]), ((), ())), precision=precision, preferred_element_type=F32
    )


def mm(left, right):
    return dot(left.astype(BF16), right.astype(BF16), ((1,), (0,)))


def mm_nt(left, right):
    return dot(left.astype(BF16), right.astype(BF16), ((1,), (1,)))


def mm_tn(left, right):
    return dot(left.astype(BF16), right.astype(BF16), ((0,), (0,)))


def softplus(v):
    return jnp.maximum(v, 0.0) + jnp.log(1.0 + jnp.exp(-jnp.abs(v)))


def sigmoid(v):
    return 1.0 / (1.0 + jnp.exp(-v))


def iotas(rows, cols):
    return (
        lax.broadcasted_iota(jnp.int32, (rows, cols), 0),
        lax.broadcasted_iota(jnp.int32, (rows, cols), 1),
    )


def unit_inverses(systems):
    if len(systems) % 2:
        pairs = [(m, m) for m in systems]
    else:
        pairs = [(systems[i], systems[i + 1]) for i in range(0, len(systems), 2)]
    rows, lanes = iotas(SPAN, 2 * SPAN)
    base = lanes - lax.rem(lanes, SPAN)
    packed = [jnp.concatenate(p, axis=1) for p in pairs]
    held = [jnp.where(rows == lax.rem(lanes, SPAN), 1.0, 0.0).astype(F32) for _ in pairs]
    for j in range(SPAN - 1):
        low = (j + 1) // 8 * 8
        for i in range(len(pairs)):
            col = jnp.take_along_axis(packed[i][low:], base[low:] + j, axis=1)
            new = held[i][low:] - col * held[i][j : j + 1]
            held[i] = jnp.concatenate([held[i][:low], new], axis=0) if low else new
    out = []
    for i in range(len(pairs)):
        out.append(held[i][:, :SPAN])
        if len(systems) % 2 == 0:
            out.append(held[i][:, SPAN:])
    return out


def gates(lg, dec_log, dec_bias):
    beta = sigmoid(lg)
    log_decay = -jnp.exp(dec_log) * softplus(lg + dec_bias)
    rows, cols = iotas(SPAN, SPAN)
    cumul = dot(jnp.where(rows >= cols, 1.0, 0.0).astype(F32), log_decay, ((1,), (0,)), HIGH)
    return beta, log_decay, cumul


def conv_act(ext, s, taps):
    total = taps[0:1] * ext[s, 5 : 5 + SPAN]
    for place in range(1, CONV):
        total = total + taps[place : place + 1] * ext[s, 5 + place : 5 + place + SPAN]
    return total


def unit_parts(act, h, heads):
    v = act[:, h * DV : (h + 1) * DV]
    a = act[:, heads * DV + h * DK : heads * DV + (h + 1) * DK]
    b = act[:, heads * (DV + DK) + h * DK : heads * (DV + DK) + (h + 1) * DK]
    qs = lax.rsqrt(jnp.sum(a * a, axis=-1, keepdims=True) + EPS)
    ks = lax.rsqrt(jnp.sum(b * b, axis=-1, keepdims=True) + EPS)
    return a, b, v, qs, ks


def decays(cumul, h, heads):
    col = cumul[:, heads + h : heads + h + 1]
    rows, cols = iotas(SPAN, SPAN)
    row = jnp.transpose(jnp.broadcast_to(col, (SPAN, SPAN)))
    spread = jnp.where(rows >= cols, jnp.broadcast_to(col, (SPAN, SPAN)) - row, 0.0)
    decay = jnp.where(rows >= cols, jnp.exp(spread), 0.0)
    growth = jnp.exp(col)
    last = col[SPAN - 1 : SPAN]
    tail = jnp.exp(last - col)
    return decay, growth, tail, jnp.exp(last), rows > cols


def fwd_body(heads, slots, held, order, comb, taps_ref, dec, hn, carry_in, state_in, *rest):
    head, mixed, t_out, s_out, u_out, carry, state, ext = rest[held:]

    @pl.when(pl.program_id(0) == 0)
    def _():
        carry[...] = carry_in[...]
        state[...] = state_in[...]

    gated, seen_by = heads * DV, heads * (2 * DV + 2 * DK)
    taps = taps_ref[...]
    units = []
    for s in range(slots):
        cur = comb[0, s, :, gated:seen_by].astype(F32)
        ext[s, 0:8] = carry[s]
        ext[s, 8 : 8 + SPAN] = cur
        carry[s] = cur[SPAN - 8 :]
        conv = conv_act(ext, s, taps)
        act = conv * sigmoid(conv)
        beta, unused, cumul = gates(comb[0, s, :, seen_by:].astype(F32), dec[0:1], dec[1:2])
        for h in range(heads):
            a, b, v, qs, ks = unit_parts(act, h, heads)
            q = (a * (qs * DK ** (-0.5))).astype(BF16)
            k32 = b * ks
            k = k32.astype(BF16)
            decay, growth, tail, last, strict = decays(cumul, h, heads)
            both = mm_nt(jnp.concatenate([q, k], axis=0), k)
            bcol = beta[:, h : h + 1]
            system = jnp.where(strict, bcol * decay * both[SPAN:], 0.0)
            scores = both[:SPAN] * decay
            units.append((s, h, q, k, k32, v, decay, growth, tail, last, bcol, system, scores))
    inverses = unit_inverses([u[11] for u in units])
    for i, (s, h, q, k, k32, v, decay, growth, tail, last, bcol, system, scores) in enumerate(units):
        inverse = inverses[i].astype(BF16)
        t_out[0, i] = inverse
        old = state[i]
        old_low = old.astype(BF16)
        s_out[0, i] = old_low
        seen = mm(jnp.concatenate([k, q], axis=0), old_low)
        target = bcol * (v - growth * seen[:SPAN])
        pseudo = mm(inverse, target).astype(BF16)
        u_out[0, i] = pseudo
        out = growth * seen[SPAN:] + mm(scores, pseudo)
        state[i] = last * old + mm_tn(k32 * tail, pseudo)
        mixed[0, s, :, h * DV : (h + 1) * DV] = out.astype(BF16)
        scale = lax.rsqrt(jnp.mean(out * out, axis=-1, keepdims=True) + EPS)
        pre = comb[0, s, :, h * DV : (h + 1) * DV].astype(F32)
        head[0, s, :, h * DV : (h + 1) * DV] = (out * scale * hn[0:1] * (pre * sigmoid(pre))).astype(BF16)


def bwd_body(
    heads, slots, left, held, order,
    comb, prev, taps_ref, dec, hn, mixed, t_in, s_in, u_in, g_head, carry_in, state_in, *rest,
):
    g_comb, g_taps, g_hn, g_dec, carry, state, ext, gext = rest[held:]
    gated, seen_by = heads * DV, heads * (2 * DV + 2 * DK)
    step = pl.program_id(0)

    @pl.when(step == 0)
    def _():
        carry[...] = carry_in[...]
        state[...] = state_in[...]
        g_taps[...] = jnp.zeros_like(g_taps)
        g_hn[...] = jnp.zeros_like(g_hn)
        g_dec[...] = jnp.zeros_like(g_dec)

    taps = taps_ref[...]
    inner = jnp.where(step == left - 1, 0.0, 1.0).astype(F32)
    rows, cols = iotas(SPAN, SPAN)
    lane = lax.broadcasted_iota(jnp.int32, (SPAN, DK), 1)
    trow = lax.broadcasted_iota(jnp.int32, (SPAN, 1), 0)
    for s in range(slots):
        cur = comb[0, s, :, gated:seen_by].astype(F32)
        logits = comb[0, s, :, seen_by:].astype(F32)
        ext[s, 0:8] = prev[0, s, SPAN - 8 :, gated:seen_by].astype(F32) * inner
        ext[s, 8 : 8 + SPAN] = cur
        conv = conv_act(ext, s, taps)
        sig = sigmoid(conv)
        act = conv * sig
        beta, log_decay, cumul = gates(logits, dec[0:1], dec[1:2])
        g_q, g_k, g_v = [], [], []
        d_beta = jnp.zeros((SPAN, DK), F32)
        d_cum = jnp.zeros((SPAN, DK), F32)
        for h in range(heads):
            i = s * heads + h
            a, b, v, qs, ks = unit_parts(act, h, heads)
            q32 = a * (qs * DK ** (-0.5))
            k32 = b * ks
            q, k = q32.astype(BF16), k32.astype(BF16)
            decay, growth, tail, last, strict = decays(cumul, h, heads)
            both = mm_nt(jnp.concatenate([q, k], axis=0), k)
            bcol = beta[:, h : h + 1]
            inverse, old, pseudo = t_in[0, i], s_in[0, i], u_in[0, i]
            scores = both[:SPAN] * decay
            span = slice(h * DV, (h + 1) * DV)
            go = g_head[0, s, :, span].astype(F32)
            pre = comb[0, s, :, span].astype(F32)
            sg = sigmoid(pre)
            out = mixed[0, s, :, span].astype(F32)
            scale = lax.rsqrt(jnp.mean(out * out, axis=-1, keepdims=True) + EPS)
            unit = out * scale
            g_comb[0, s, :, span] = (go * unit * hn[0:1] * (sg * (1.0 + pre * (1.0 - sg)))).astype(BF16)
            up = go * (pre * sg)
            g_hn[0:1] += jnp.sum(up * unit, axis=0, keepdims=True)
            e = up * hn[0:1]
            d_out = scale * (e - unit * jnp.mean(e * unit, axis=-1, keepdims=True))
            d_out_low = d_out.astype(BF16)
            d_next = state[i]
            d_next_low = d_next.astype(BF16)
            d_pseudo = mm_tn(scores, d_out_low) + mm(k32 * tail, d_next_low)
            d_right = mm_tn(inverse, d_pseudo)
            d_right_low = d_right.astype(BF16)
            both_g = jnp.concatenate([d_out_low, d_right_low], axis=0)
            state[i] = last * d_next + mm_tn(
                jnp.concatenate([growth * q32, -(growth * bcol) * k32], axis=0), both_g
            )
            by_state = mm_nt(both_g, old)
            by_pseudo = mm_nt(both_g, pseudo)
            out_state, right_state = by_state[:SPAN], by_state[SPAN:]
            tail_state = mm_nt(pseudo, d_next_low)
            d_scores = by_pseudo[:SPAN]
            d_system = jnp.where(strict, -by_pseudo[SPAN:], 0.0)
            d_att = d_scores * decay
            d_inter = d_system * decay
            square = d_att * both[:SPAN] + d_inter * both[SPAN:] * bcol
            pair = jnp.concatenate([d_att, d_inter * bcol], axis=0)
            first = mm(pair, k)
            second = mm_tn(pair, jnp.concatenate([q, k], axis=0))
            out_q = growth * jnp.sum(out_state * q32, axis=-1, keepdims=True)
            right_k = growth * jnp.sum(right_state * k32, axis=-1, keepdims=True)
            tail_k = tail * jnp.sum(tail_state * k32, axis=-1, keepdims=True)
            dq = growth * out_state + first[:SPAN]
            dk = first[SPAN:] + second - (growth * bcol) * right_state + tail * tail_state
            dv = bcol * d_right
            db = (
                jnp.sum(d_right * v, axis=-1, keepdims=True)
                - right_k
                + jnp.sum(d_inter * both[SPAN:], axis=-1, keepdims=True)
            )
            dc = (
                jnp.sum(square - jnp.transpose(square), axis=-1, keepdims=True)
                + out_q
                - bcol * right_k
                - tail_k
            )
            at_last = jnp.sum(tail_k, axis=0, keepdims=True) + last * jnp.sum(
                jnp.sum(d_next * old.astype(F32), axis=-1, keepdims=True), axis=0, keepdims=True
            )
            dc = dc + jnp.where(trow == SPAN - 1, at_last, 0.0)
            d_beta = jnp.where(lane == h, db, d_beta)
            d_cum = jnp.where(lane == heads + h, dc, d_cum)
            qh = a * qs
            g_q.append((qs * DK ** (-0.5)) * (dq - qh * jnp.sum(qh * dq, axis=-1, keepdims=True)))
            g_k.append(ks * (dk - k32 * jnp.sum(k32 * dk, axis=-1, keepdims=True)))
            g_v.append(dv)
        d_log = dot(jnp.where(cols >= rows, 1.0, 0.0).astype(F32), d_cum, ((1,), (0,)), HIGH)
        pre_gate = logits + dec[1:2]
        d_alpha = d_log * (-jnp.exp(dec[0:1])) * sigmoid(pre_gate)
        g_dec[0:1] += jnp.sum(d_log * log_decay, axis=0, keepdims=True)
        g_dec[1:2] += jnp.sum(d_alpha, axis=0, keepdims=True)
        g_comb[0, s, :, seen_by:] = (d_beta * beta * (1.0 - beta) + d_alpha).astype(BF16)
        g_act = jnp.concatenate(g_v + g_q + g_k, axis=1)
        g_conv = g_act * (sig * (1.0 + conv * (1.0 - sig)))
        gext[s, 0:SPAN] = g_conv
        gext[s, SPAN : SPAN + 8] = carry[s]
        carry[s] = g_conv[0:8]
        total = taps[CONV - 1 : CONV] * g_conv
        for place in range(CONV):
            g_taps[place : place + 1] += jnp.sum(
                g_conv * ext[s, 5 + place : 5 + place + SPAN], axis=0, keepdims=True
            )
            if place < CONV - 1:
                total = total + taps[place : place + 1] * gext[s, CONV - 1 - place : CONV - 1 - place + SPAN]
        g_comb[0, s, :, gated:seen_by] = total.astype(BF16)


def geometry(comb):
    shards, slots, seg, wide = comb.shape
    heads = (wide - DK) // (2 * DK + 2 * DV)
    return shards, slots, seg, heads, seg // SPAN, wide


def token_spec(slots, width, per, at):
    return pl.BlockSpec((1, slots, SPAN, width), lambda n, order: (at(n) // per, 0, lax.rem(at(n), per), 0))


def placed_spec(slots, width, per, at):
    return pl.BlockSpec(
        (1, slots, SPAN, width), lambda n, order: (order[at(n) // per], 0, lax.rem(at(n), per), 0)
    )


def fixed_spec(*shape):
    return pl.BlockSpec(shape, lambda n, order: (0,) * len(shape))


def no_links(slots, heads):
    return [jnp.zeros((slots, 8, heads * (2 * DK + DV)), F32), jnp.zeros((slots * heads, DK, DV), F32)]


def mix_forward(first, steps, held, links, order, comb, taps, dec, hn):
    shards, slots, seg, heads, per, wide = geometry(comb)
    spans, chains, chans = shards * per, slots * heads, heads * (2 * DK + DV)
    at = lambda n: n + first
    tok = lambda width: token_spec(slots, width, per, at)
    unit = lambda *shape: pl.BlockSpec((1, chains) + shape, lambda n, order: (at(n), 0, 0, 0))
    links = links or no_links(slots, heads)
    done = pl.pallas_call(
        functools.partial(fwd_body, heads, slots, len(held)),
        grid_spec=pltpu.PrefetchScalarGridSpec(
            num_scalar_prefetch=1,
            grid=(steps,),
            in_specs=[tok(wide)]
            + [fixed_spec(*a.shape) for a in (taps, dec, hn, *links)]
            + [pl.BlockSpec(memory_space=pl.ANY)] * len(held),
            out_specs=[
                placed_spec(slots, heads * DV, per, at), tok(heads * DV),
                unit(SPAN, SPAN), unit(DK, DV), unit(SPAN, DV),
                fixed_spec(slots, 8, chans), fixed_spec(chains, DK, DV),
            ],
            scratch_shapes=[pltpu.VMEM((slots, SPAN + 8, chans), F32)],
        ),
        out_shape=[
            jax.ShapeDtypeStruct((shards, slots, seg, heads * DV), BF16),
            jax.ShapeDtypeStruct((shards, slots, seg, heads * DV), BF16),
            jax.ShapeDtypeStruct((spans, chains, SPAN, SPAN), BF16),
            jax.ShapeDtypeStruct((spans, chains, DK, DV), BF16),
            jax.ShapeDtypeStruct((spans, chains, SPAN, DV), BF16),
            jax.ShapeDtypeStruct((slots, 8, chans), F32),
            jax.ShapeDtypeStruct((chains, DK, DV), F32),
        ],
        input_output_aliases={7 + i: i for i in range(len(held))},
        compiler_params=pltpu.CompilerParams(vmem_limit_bytes=40 << 20),
        cost_estimate=pl.CostEstimate(
            flops=steps * chains * 600_000_000, bytes_accessed=steps * chains * 400_000, transcendentals=0
        ),
        name="mix_forward",
    )(order, comb, taps, dec, hn, *links, *held)
    return list(done[:5]), list(done[5:])


def mix_backward(first, steps, held, links, order, comb, taps, dec, hn, saved, g_head):
    shards, slots, seg, heads, per, wide = geometry(comb)
    spans, chains, chans = shards * per, slots * heads, heads * (2 * DK + DV)
    last = spans - 1 - first
    back = lambda n: last - n
    tok = lambda width: token_spec(slots, width, per, back)
    before = token_spec(slots, wide, per, lambda n: jnp.maximum(last - 1 - n, 0))
    unit = lambda *shape: pl.BlockSpec((1, chains) + shape, lambda n, order: (back(n), 0, 0, 0))
    links = links or no_links(slots, heads)
    done = pl.pallas_call(
        functools.partial(bwd_body, heads, slots, last + 1, len(held)),
        grid_spec=pltpu.PrefetchScalarGridSpec(
            num_scalar_prefetch=1,
            grid=(steps,),
            in_specs=[tok(wide), before]
            + [fixed_spec(*a.shape) for a in (taps, dec, hn)]
            + [tok(heads * DV), unit(SPAN, SPAN), unit(DK, DV), unit(SPAN, DV)]
            + [placed_spec(slots, heads * DV, per, back)]
            + [fixed_spec(*a.shape) for a in links]
            + [pl.BlockSpec(memory_space=pl.ANY)] * len(held),
            out_specs=[
                tok(wide), fixed_spec(8, chans), fixed_spec(8, DV), fixed_spec(8, DK),
                fixed_spec(slots, 8, chans), fixed_spec(chains, DK, DV),
            ],
            scratch_shapes=[
                pltpu.VMEM((slots, SPAN + 8, chans), F32),
                pltpu.VMEM((slots, SPAN + 8, chans), F32),
            ],
        ),
        out_shape=[
            jax.ShapeDtypeStruct(comb.shape, BF16),
            jax.ShapeDtypeStruct((8, chans), F32),
            jax.ShapeDtypeStruct((8, DV), F32),
            jax.ShapeDtypeStruct((8, DK), F32),
            jax.ShapeDtypeStruct((slots, 8, chans), F32),
            jax.ShapeDtypeStruct((chains, DK, DV), F32),
        ],
        input_output_aliases={13 + i: i for i in range(len(held))},
        compiler_params=pltpu.CompilerParams(vmem_limit_bytes=40 << 20),
        cost_estimate=pl.CostEstimate(
            flops=steps * chains * 900_000_000, bytes_accessed=steps * chains * 600_000, transcendentals=0
        ),
        name="mix_backward",
    )(order, comb, comb, taps, dec, hn, *saved, g_head, *links, *held)
    return list(done[:1]), list(done[1:4]), list(done[4:])


HEADS = 16
FAR, NEAR = 4, 2
COPIES = 4


def taken(items, index):
    return lax.dynamic_index_in_dim(items, index, 0, keepdims=False)


def placed_at(items, item, index):
    return lax.dynamic_update_slice_in_dim(items, item[None], index, 0)


def low_sum(*terms):
    total = terms[0].astype(F32)
    for term in terms[1:]:
        total = total + term.astype(F32)
    return total.astype(BF16)


class Flow(dict):
    def step(self):
        names = list(self)
        leaves, tree = jax.tree.flatten([self[name] for name in names])
        self.update(zip(names, jax.tree.unflatten(tree, lax.optimization_barrier(tuple(leaves)))))

    def take(self, *names):
        got = [self.pop(name) for name in names]
        return got[0] if len(got) == 1 else got


def split_columns(step_rows, cut, gain, starts, weight, out):
    group = out.shape[2] // 4
    window = group + 128
    lanes = lax.broadcasted_iota(jnp.int32, (step_rows, group), 1)
    for side in range(2):
        for place in range(4):
            total = jnp.zeros((step_rows, group), F32)
            for half in range(2):
                start = starts[side, 2 * place + half]
                low = jnp.minimum(start // 128 * 128, weight.shape[1] - window)
                seen = weight[:, pl.ds(pl.multiple_of(low, 128), window)].astype(F32)
                shift = lax.rem(half * cut - (start - low) + window, window)
                moved = pltpu.roll(seen, shift, 1)[:, :group]
                keep = (lanes >= half * cut) & (lanes < (half + 1) * cut)
                total = jnp.where(keep, moved, total)
            out[side, :, place * group : (place + 1) * group] = (total * gain[...]).astype(BF16)


def pick_columns(weight, gain, starts, cut, group):
    rows, step = weight.shape[0], 64
    return pl.pallas_call(
        lambda starts, weight, gain, out: split_columns(step, cut, gain, starts, weight, out),
        grid_spec=pltpu.PrefetchScalarGridSpec(
            num_scalar_prefetch=1,
            grid=(rows // step,),
            in_specs=[
                pl.BlockSpec((step, weight.shape[1]), lambda n, starts: (n, 0)),
                pl.BlockSpec((step, 1), lambda n, starts: (n, 0)),
            ],
            out_specs=pl.BlockSpec((2, step, 4 * group), lambda n, starts: (0, n, 0)),
        ),
        out_shape=jax.ShapeDtypeStruct((2, rows, 4 * group), BF16),
        compiler_params=pltpu.CompilerParams(vmem_limit_bytes=40 << 20),
        name="pick_columns",
    )(starts, weight, gain)


def merge_body(cut, group, copy, parts, weight, gain, grad, dots):
    total = 0.0
    span = NEAR * COPIES * cut
    for which in range(2):
        for far in range(FAR):
            at = which * 2 * group + far // 2 * group + far % 2 * cut
            pieces = [
                parts[index ^ copy[0], near, :, at : at + cut].astype(F32)
                for near in range(NEAR)
                for index in range(COPIES)
            ]
            joined = jnp.concatenate(pieces, axis=1)
            here = pl.ds((which * FAR + far) * span, span)
            grad[:, here] = joined * gain[...]
            total = total + jnp.sum(weight[:, here].astype(F32) * joined, axis=1, keepdims=True)
    dots[...] = jnp.broadcast_to(total, dots.shape)


def merge_columns(copy, parts, weight, gain, cut, group):
    rows, cols, step = weight.shape[0], weight.shape[1], 32
    return pl.pallas_call(
        functools.partial(merge_body, cut, group),
        grid_spec=pltpu.PrefetchScalarGridSpec(
            num_scalar_prefetch=1,
            grid=(rows // step,),
            in_specs=[
                pl.BlockSpec((COPIES, NEAR, step, parts.shape[3]), lambda n, copy: (0, 0, n, 0)),
                pl.BlockSpec((step, cols), lambda n, copy: (n, 0)),
                pl.BlockSpec((step, 1), lambda n, copy: (n, 0)),
            ],
            out_specs=[
                pl.BlockSpec((step, cols), lambda n, copy: (n, 0)),
                pl.BlockSpec((step, 128), lambda n, copy: (n, 0)),
            ],
        ),
        out_shape=[jax.ShapeDtypeStruct((rows, cols), F32), jax.ShapeDtypeStruct((rows, 128), F32)],
        compiler_params=pltpu.CompilerParams(vmem_limit_bytes=40 << 20),
        name="merge_columns",
    )(copy, parts, weight, gain)


def pack_body(heads, copy, gate, value, query, key, ab, gain, out):
    device = pl.program_id(0)
    scaled = lambda weight: (weight[...].astype(F32) * gain[...]).astype(BF16)
    wide, narrow = heads * DV, heads * DK
    out[0, :, :wide] = scaled(gate)
    out[0, :, wide : 2 * wide] = scaled(value)
    out[0, :, 2 * wide : 2 * wide + narrow] = scaled(query)
    out[0, :, 2 * wide + narrow : 2 * wide + 2 * narrow] = scaled(key)
    both = ab[...].astype(F32) * gain[...]
    lanes = lax.broadcasted_iota(jnp.int32, both.shape, 1)
    strength = pltpu.roll(both, lax.rem(DK - heads * device, DK), 1)
    decay = pltpu.roll(both, lax.rem(DK + heads - HEADS - heads * device, DK), 1)
    out[0, :, 2 * wide + 2 * narrow :] = jnp.where(
        lanes < heads, strength, jnp.where(lanes < 2 * heads, decay, 0.0)
    ).astype(BF16)


def pack_mixer(copy, mixer_in, gate_weight, alpha_beta, gain):
    devices = FAR * NEAR
    heads, rows = HEADS // devices, mixer_in.shape[0] // COPIES
    wide, narrow = heads * DV, heads * DK
    total = 2 * wide + 2 * narrow + DK
    ab = jnp.pad(alpha_beta, ((0, 0), (0, DK - 2 * HEADS)))
    return pl.pallas_call(
        functools.partial(pack_body, heads),
        grid_spec=pltpu.PrefetchScalarGridSpec(
            num_scalar_prefetch=1,
            grid=(devices,),
            in_specs=[
                pl.BlockSpec((rows, wide), lambda d, copy: (copy[0], d)),
                pl.BlockSpec((rows, wide), lambda d, copy: (copy[0], devices + d)),
                pl.BlockSpec((rows, narrow), lambda d, copy: (copy[0], d)),
                pl.BlockSpec((rows, narrow), lambda d, copy: (copy[0], devices + d)),
                pl.BlockSpec((rows, DK), lambda d, copy: (copy[0], 0)),
                pl.BlockSpec((rows, 1), lambda d, copy: (copy[0], 0)),
            ],
            out_specs=pl.BlockSpec((1, rows, total), lambda d, copy: (d, 0, 0)),
        ),
        out_shape=jax.ShapeDtypeStruct((devices, rows, total), BF16),
        compiler_params=pltpu.CompilerParams(vmem_limit_bytes=40 << 20),
        name="pack_mixer",
    )(copy, gate_weight, mixer_in, mixer_in, mixer_in, ab, gain)


def unpack_body(devices, copy, wide_in, left, right, w_in, w_gate, gain, g_in, g_gate, dots):
    step = pl.program_id(0)

    def whole(ref):
        return jnp.concatenate([ref[index ^ copy[0], 0] for index in range(COPIES)], axis=0).astype(F32)

    def put(grad, weight, out):
        out[...] = grad * gain[...]
        total = jnp.sum(weight[...].astype(F32) * grad, axis=1, keepdims=True)
        dots[...] += jnp.broadcast_to(total, dots.shape)

    @pl.when(step == 0)
    def _():
        dots[...] = jnp.zeros_like(dots)

    @pl.when(step < devices)
    def _():
        put(jnp.concatenate([whole(left), whole(right)], axis=1), w_in, g_in)

    @pl.when((step >= devices) & (step < 2 * devices))
    def _():
        put(whole(wide_in), w_in, g_in)

    @pl.when(step >= 2 * devices)
    def _():
        put(whole(wide_in), w_gate, g_gate)


def unpack_mixer(copy, first, second, mixer_in, gate_weight, gain):
    devices = FAR * NEAR
    heads, rows = HEADS // devices, mixer_in.shape[0]
    wide, narrow, quarter = heads * DV, heads * DK, rows // COPIES
    low = lambda n: jnp.minimum(n, devices - 1)

    def side(which):
        def index(n, copy):
            kind, pair = low(n) // (devices // 2), lax.rem(low(n), devices // 2)
            return 0, 2 * pair + which, 0, kind

        return pl.BlockSpec((COPIES, 1, quarter, narrow), index)

    def wide_index(n, copy):
        past = jnp.maximum(n - devices, 0)
        return 0, lax.rem(past, devices), 0, 1 - past // devices

    into = lambda n, copy: (0, jnp.minimum(n, 2 * devices - 1))
    gates = lambda n, copy: (0, jnp.maximum(n - 2 * devices, 0))
    return pl.pallas_call(
        functools.partial(unpack_body, devices),
        grid_spec=pltpu.PrefetchScalarGridSpec(
            num_scalar_prefetch=1,
            grid=(3 * devices,),
            in_specs=[
                pl.BlockSpec((COPIES, 1, quarter, wide), wide_index),
                side(0),
                side(1),
                pl.BlockSpec((rows, wide), into),
                pl.BlockSpec((rows, wide), gates),
                pl.BlockSpec((rows, 1), lambda n, copy: (0, 0)),
            ],
            out_specs=[
                pl.BlockSpec((rows, wide), into),
                pl.BlockSpec((rows, wide), gates),
                pl.BlockSpec((rows, 128), lambda n, copy: (0, 0)),
            ],
        ),
        out_shape=[
            jax.ShapeDtypeStruct(mixer_in.shape, F32),
            jax.ShapeDtypeStruct(gate_weight.shape, F32),
            jax.ShapeDtypeStruct((rows, 128), F32),
        ],
        compiler_params=pltpu.CompilerParams(vmem_limit_bytes=40 << 20),
        name="unpack_mixer",
    )(copy, first, second, second, mixer_in, gate_weight, gain)


class Lines:
    def __init__(self):
        self.count, self.copies = lax.axis_size("shard"), lax.axis_size("rep")
        self.me, self.copy = lax.axis_index("shard"), lax.axis_index("rep")
        self.known = self.count == FAR * NEAR and self.copies == COPIES
        far = self.far = self.me // NEAR
        self.near = lax.rem(self.me, NEAR)
        self.chip, self.core = self.copy // 2, lax.rem(self.copy, 2)
        self.rows = (
            far,
            jnp.where(far == 0, 1, far - 1),
            jnp.where(far == 0, 2, jnp.where(far == 3, 1, far + 1)),
            jnp.where(far < 2, 3, 0),
        )

    def along(self, item, sources, by):
        return lax.ppermute(
            item, "shard", [(2 * z + y, 2 * (z + by) + y) for z in sources for y in range(2)]
        )

    def turned(self, item, by):
        return lax.ppermute(
            item, "shard", [(2 * z + y, 2 * ((z + by) % FAR) + y) for z in range(FAR) for y in range(2)]
        )

    def over(self, item):
        return lax.ppermute(item, "shard", [(i, i ^ 1) for i in range(FAR * NEAR)])

    def crossed(self, item, bit):
        return lax.ppermute(item, "shard", [(i, i ^ bit) for i in range(FAR * NEAR)])

    def to_core(self, item):
        return lax.ppermute(item, "rep", [(i, i ^ 1) for i in range(COPIES)])

    def to_chip(self, item):
        return lax.ppermute(item, "rep", [(i, i ^ 2) for i in range(COPIES)])

    def order(self):
        device = lax.iota(jnp.int32, FAR * NEAR)
        row, place = device // NEAR, jnp.zeros((FAR * NEAR,), jnp.int32)
        for index in range(1, FAR):
            place = jnp.where(row == self.rows[index], index, place)
        return (NEAR * place + (lax.rem(device, NEAR) ^ self.near)).astype(jnp.int32)

    def out_1(self, piece):
        return self.along(piece, (0, 1, 2), 1), self.along(piece, (1, 2, 3), -1)

    def out_2(self, got_1):
        return self.along(got_1[0], (1, 2), 1), self.along(got_1[1], (2, 1), -1)

    def ends(self, item, outward):
        pairs = [(1, 0), (2, 3)] if outward else [(0, 1), (3, 2)]
        return lax.ppermute(item, "shard", [(2 * a + y, 2 * b + y) for a, b in pairs for y in range(2)])

    def out_3(self, got_2):
        return self.ends(jnp.where(self.far == 1, got_2[1], got_2[0]), True)

    def line_1(self, got_1):
        return jnp.where(self.far == 0, got_1[1], got_1[0])

    def line_2(self, got_1, got_2):
        return jnp.where(self.far == 0, got_2[1], jnp.where(self.far == 3, got_2[0], got_1[1]))

    def line_3(self, got_2, got_3):
        far = self.far
        return jnp.where(far == 1, got_2[1], jnp.where(far == 2, got_2[0], got_3))

    def line_whole(self, piece, got_1, got_2, got_3):
        pieces = (piece, self.line_1(got_1), self.line_2(got_1, got_2), self.line_3(got_2, got_3))
        whole = jnp.zeros((FAR,) + piece.shape, piece.dtype)
        for row, item in zip(self.rows, pieces):
            whole = placed_at(whole, item, row)
        return whole

    def in_3(self, sum_3):
        return self.ends(sum_3, False)

    def in_2(self, sum_3, got_3, sum_2):
        passed = low_sum(sum_3, got_3)
        up = jnp.where(self.far == 3, sum_2, passed)
        down = jnp.where(self.far == 0, sum_2, passed)
        return self.along(up, (3, 2), -1), self.along(down, (0, 1), 1)

    def in_1(self, sum_2, got_2, sum_1):
        down = jnp.where(self.far == 0, sum_1, low_sum(sum_2, got_2[1]))
        return self.along(low_sum(sum_1, got_2[0]), (3, 2, 1), -1), self.along(down, (0, 1, 2), 1)

    def sum_0(self, own, got_1):
        return own.astype(F32) + got_1[0].astype(F32) + got_1[1].astype(F32)

    def own_quarter(self, rows):
        size = rows.shape[0] // self.copies
        return lax.dynamic_slice_in_dim(rows, self.copy * size, size, 0)

    def quarters(self, own, by_core, by_chip, by_both):
        chip, core = self.chip, self.core
        whole = jnp.zeros((COPIES,) + own.shape, own.dtype)
        whole = placed_at(whole, own, 2 * chip + core)
        whole = placed_at(whole, by_core, 2 * chip + 1 - core)
        whole = placed_at(whole, by_chip, 2 * (1 - chip) + core)
        return placed_at(whole, by_both, 2 * (1 - chip) + 1 - core)


def rms_back(values, scale, grad):
    mean = jnp.mean(grad * values, axis=-1, keepdims=True)
    return scale * grad - values * (scale * scale * scale) * mean


def rms_rate(values):
    return lax.rsqrt(jnp.mean(values * values, axis=-1, keepdims=True) + EPS)


class Small:
    def __init__(self, lines, conv_taps, head_norm):
        self.shards, self.me = lines.count, lines.me
        self.heads = HEADS // self.shards
        self.chan_part, self.gain_part = conv_taps.shape[1], head_norm.shape[0]
        self.narrow, self.wide = self.heads * DK, self.heads * DV
        self.chans = 2 * self.narrow + self.wide

    def parameters(self, gathered):
        taps = gathered[:, : CONV * self.chan_part].reshape(self.shards, CONV, self.chan_part)
        taps = jnp.moveaxis(taps, 0, 1).reshape(CONV, self.shards * self.chan_part)
        gain = jnp.broadcast_to(gathered[:, CONV * self.chan_part :].reshape(1, DV), (8, DV))
        key_width, first = HEADS * DK, self.me * self.heads
        taps = jnp.concatenate(
            [
                lax.dynamic_slice_in_dim(taps, 2 * key_width + first * DV, self.wide, 1),
                lax.dynamic_slice_in_dim(taps, first * DK, self.narrow, 1),
                lax.dynamic_slice_in_dim(taps, key_width + first * DK, self.narrow, 1),
            ],
            axis=1,
        )
        return jnp.pad(taps, ((0, 8 - CONV), (0, 0))), gain

    def decay(self, decay_log, decay_bias):
        def own(item):
            item = lax.dynamic_slice_in_dim(item, self.me * self.heads, self.heads, 0)
            return jnp.pad(item, (self.heads, DK - 2 * self.heads))

        return jnp.pad(jnp.stack([own(decay_log), own(decay_bias)]), ((0, 6), (0, 0)))

    def terms(self, g_taps, g_gain, g_decay):
        alpha = slice(self.heads, 2 * self.heads)
        return jnp.concatenate([g_taps[:CONV].reshape(-1), g_gain[0], g_decay[0, alpha], g_decay[1, alpha]])

    def gradients(self, gathered):
        end = CONV * self.chans
        taps = gathered[:, :end].reshape(self.shards, CONV, self.chans)
        taps = jnp.concatenate(
            [
                jnp.moveaxis(item, 0, 1).reshape(CONV, -1)
                for item in (
                    taps[:, :, self.wide : self.wide + self.narrow],
                    taps[:, :, self.wide + self.narrow :],
                    taps[:, :, : self.wide],
                )
            ],
            axis=1,
        )
        taps = lax.dynamic_slice_in_dim(taps, self.me * self.chan_part, self.chan_part, 1)
        gain = jnp.sum(gathered[:, end : end + DV], axis=0)
        gain = lax.dynamic_slice_in_dim(gain, self.me * self.gain_part, self.gain_part, 0)
        at = end + DV
        return taps, gain, gathered[:, at : at + self.heads].reshape(-1), gathered[:, at + self.heads :].reshape(-1)


def fanned(weight, shards):
    return jnp.moveaxis(weight.reshape(weight.shape[0], shards, -1), 1, 0)


def mixer_parts(mixer_rows, gate_rows, ab_rows, shards):
    key_width, heads = HEADS * DK, HEADS // shards
    ab = jnp.concatenate([fanned(ab_rows[:, :HEADS], shards), fanned(ab_rows[:, HEADS:], shards)], axis=2)
    return jnp.concatenate(
        [
            fanned(gate_rows, shards),
            fanned(mixer_rows[:, 2 * key_width :], shards),
            fanned(mixer_rows[:, :key_width], shards),
            fanned(mixer_rows[:, key_width : 2 * key_width], shards),
            jnp.pad(ab, ((0, 0), (0, 0), (0, DK - 2 * heads))),
        ],
        axis=2,
    )


def mixer_grads(small, owned, mixer_norm, mixer_in, gate_weight, alpha_beta):
    rows, heads = mixer_in.shape[0], small.heads
    gain = mixer_norm.astype(F32)[:, None]

    def joined(low, high):
        return jnp.moveaxis(owned[:, :, low:high], 0, 1).reshape(rows, -1).astype(F32)

    def with_gain(weight, grad):
        return gain * grad, jnp.sum(weight.astype(F32) * grad, axis=1)

    query = 2 * small.wide
    key, ab = query + small.narrow, query + 2 * small.narrow
    g_in = [joined(query, key), joined(key, ab), joined(small.wide, query)]
    g_in, norm_a = with_gain(mixer_in, jnp.concatenate(g_in, axis=1))
    g_gate, norm_b = with_gain(gate_weight, joined(0, small.wide))
    g_ab = jnp.concatenate([joined(ab, ab + heads), joined(ab + heads, ab + 2 * heads)], axis=1)
    g_ab, norm_c = with_gain(alpha_beta, g_ab)
    return norm_a + norm_b + norm_c, g_in, g_gate, g_ab


def masked(out_cotangent, slot_length, me):
    slots, seg, unused = out_cotangent.shape
    positions = me * seg + lax.broadcasted_iota(jnp.int32, (slots, seg), 1)
    return out_cotangent.astype(F32) * (positions < slot_length[:, None]).astype(F32)[..., None]


def feed_forward(pre, g_hidden):
    half = pre.shape[1] // 2
    u, w = pre[:, :half].astype(F32), pre[:, half:].astype(F32)
    sig = sigmoid(u)
    g_u = g_hidden * w * (sig * (1.0 + u * (1.0 - sig)))
    return (u * sig * w).astype(BF16), jnp.concatenate([g_u, g_hidden * (u * sig)], axis=1).astype(BF16)


def on_device(
    inputs, out_cotangent, slot_length, mixer_norm, mixer_in, gate_weight, alpha_beta, conv_taps,
    decay_log, decay_bias, head_norm, mixer_out, feed_norm, gate_up, down_weight,
):
    lines = Lines()
    run = on_known if lines.known else on_any
    return run(
        lines, Small(lines, conv_taps, head_norm),
        inputs, out_cotangent, slot_length, mixer_norm, mixer_in, gate_weight, alpha_beta, conv_taps,
        decay_log, decay_bias, head_norm, mixer_out, feed_norm, gate_up, down_weight,
    )


def on_any(
    lines, small,
    inputs, out_cotangent, slot_length, mixer_norm, mixer_in, gate_weight, alpha_beta, conv_taps,
    decay_log, decay_bias, head_norm, mixer_out, feed_norm, gate_up, down_weight,
):
    shards = lines.count
    slots, seg, width = inputs.shape
    rows, ff = mixer_in.shape[0], down_weight.shape[0]
    flat = lambda item: item.reshape((shards * slots * seg,) + item.shape[3:])
    unflat = lambda item: item.reshape((shards, slots, seg) + item.shape[1:])
    gather = lambda item: lax.all_gather(item, "shard", axis=0)
    scatter = lambda item: lax.psum_scatter(unflat(item.astype(BF16)), "shard", scatter_dimension=0, tiled=False).astype(F32)
    swap = lambda item: lax.all_to_all(item, "shard", 0, 0)
    gain_in, gain_feed = mixer_norm.astype(F32)[:, None], feed_norm.astype(F32)[:, None]
    scaled = lambda weight, gain: (weight.astype(F32) * gain).astype(BF16)
    taps, gain = small.parameters(gather(jnp.concatenate([conv_taps.reshape(-1), head_norm])).astype(F32))
    decay = small.decay(decay_log, decay_bias)
    w_mixer = swap(mixer_parts(scaled(mixer_in, gain_in), scaled(gate_weight, gain_in), scaled(alpha_beta, gain_in), shards))
    w_mixer = w_mixer.reshape(width, -1)
    up_rows = scaled(gate_up, gain_feed).reshape(rows, 2, shards, ff)
    w_up = swap(jnp.transpose(up_rows, (2, 0, 1, 3))).reshape(width, 2 * ff)
    x = inputs.astype(F32)
    x_rate = rms_rate(x)
    x_all = flat(gather((x * x_rate).astype(BF16)))
    comb = unflat(mm(x_all, w_mixer).astype(BF16))
    order = lax.iota(jnp.int32, shards)
    spans = shards * seg // SPAN
    held, unused = mix_forward(0, spans, [], None, order, comb, taps, decay, gain)
    g_out = masked(out_cotangent, slot_length, lines.me)
    g_out_all = flat(gather(g_out.astype(BF16)))
    resid = x + scatter(mm(flat(held[0]), mixer_out))
    rate = rms_rate(resid)
    feed_all = flat(gather((resid * rate).astype(BF16)))
    hidden, g_pre = feed_forward(mm(feed_all, w_up).astype(BF16), mm_nt(g_out_all, down_weight))
    layer_out = (resid + scatter(mm(hidden, down_weight))).astype(BF16)
    g_resid = g_out + rms_back(resid, rate, scatter(mm_nt(g_pre, w_up)))
    g_resid_all = flat(gather(g_resid.astype(BF16)))
    g_head = unflat(mm_nt(g_resid_all, mixer_out).astype(BF16))
    grads, terms, unused = mix_backward(0, spans, [], None, order, comb, taps, decay, gain, held[1:], g_head)
    g_mixer = flat(grads[0])
    input_grad = (g_resid + rms_back(x, x_rate, scatter(mm_nt(g_mixer, w_mixer)))).astype(BF16)
    total = lambda item: lax.psum(item.astype(BF16), "rep").astype(F32)
    owned = swap(total(mm_tn(x_all, g_mixer)).astype(BF16).reshape(shards, rows, -1))
    g_norm, g_in, g_gate, g_ab = mixer_grads(small, owned, mixer_norm, mixer_in, gate_weight, alpha_beta)
    up_owned = swap(total(mm_tn(feed_all, g_pre)).astype(BF16).reshape(shards, rows, 2, ff)).astype(F32)
    up_owned = jnp.transpose(up_owned, (1, 2, 0, 3)).reshape(rows, -1)
    g_feed_norm = jnp.sum(up_owned * gate_up.astype(F32), axis=1)
    g_taps, g_gain, g_log, g_bias = small.gradients(gather(lax.psum(small.terms(*terms), "rep")))
    return (
        layer_out, input_grad, g_norm, g_in, g_gate, g_ab, g_taps, g_log, g_bias, g_gain,
        total(mm_tn(flat(held[0]), g_resid_all)), g_feed_norm, gain_feed * up_owned, total(mm_tn(hidden, g_out_all)),
    )


def on_known(
    lines, small,
    inputs, out_cotangent, slot_length, mixer_norm, mixer_in, gate_weight, alpha_beta, conv_taps,
    decay_log, decay_bias, head_norm, mixer_out, feed_norm, gate_up, down_weight,
):
    far, near, copies = lines.far, lines.near, COPIES
    slots, seg, width = inputs.shape
    piece = slots * seg
    rows, ff = mixer_in.shape[0], down_weight.shape[0]
    chans, wide = small.chans, small.wide
    flat = lambda item: item.reshape((-1,) + item.shape[3:])
    unflat = lambda item: item.reshape((-1, slots, seg) + item.shape[1:])
    at = lambda item, *places: jnp.concatenate([item[p] for p in places]) if len(places) > 1 else item[places[0]]
    f = Flow()
    copy = lines.copy.astype(jnp.int32)[None]

    x = inputs.astype(F32)
    x_all = lax.all_gather((x * rms_rate(x)).astype(BF16), "shard", axis=0)
    gain_in, gain_feed = mixer_norm.astype(F32)[:, None], feed_norm.astype(F32)[:, None]
    f["quarter"] = lax.all_to_all(pack_mixer(copy, mixer_in, gate_weight, alpha_beta, gain_in), "shard", 0, 0)
    f["small"] = jnp.concatenate([conv_taps.reshape(-1), head_norm])[None]
    f["small_1"] = lines.crossed(f["small"], 1)
    f.step()

    f["by_core"], f["by_chip"] = lines.to_core(f["quarter"]), lines.to_chip(f["quarter"])
    f["small"] = jnp.concatenate([f["small"], f.take("small_1")])
    f["small_1"] = lines.crossed(f["small"], 2)
    cut = ff // copies
    group = (2 * cut + 127) // 128 * 128
    half_ff = 2 * group
    sides = jnp.stack([near, 1 - near])[:, None]
    blocks = jnp.arange(2 * FAR)
    starts = blocks // FAR * (FAR * NEAR * ff) + ff * (NEAR * (blocks % FAR) + sides) + cut * lines.copy
    f["picked"] = pick_columns(gate_up, gain_feed, starts.astype(jnp.int32), cut, group)
    f["g_low"] = masked(out_cotangent, slot_length, lines.me).astype(BF16)
    f["down"] = lines.own_quarter(down_weight)
    f.step()

    f["by_both"] = lines.to_core(f["by_chip"])
    f["small"] = jnp.concatenate([f["small"], f.take("small_1")])
    f["small_1"] = lines.crossed(f["small"], 4)
    f["up_over"] = lines.over(f["picked"][1])
    f.step()

    w_mixer = lines.quarters(*f.take("quarter", "by_core", "by_chip", "by_both"))
    f["w_mixer"] = jnp.moveaxis(w_mixer, 0, 1).reshape(width, -1)
    ordered = jnp.take(
        jnp.concatenate([f.take("small"), f.take("small_1")]), lax.iota(jnp.int32, FAR * NEAR) ^ lines.me, axis=0
    )
    f["taps"], f["gain"] = small.parameters(ordered.astype(F32))
    f["decay"] = small.decay(decay_log, decay_bias)
    f["order"] = lines.order()
    own, other = f.take("picked")[0], f.take("up_over")
    f["up"] = jnp.where(near == 0, jnp.stack([own, other]), jnp.stack([other, own]))
    f["x_all"] = flat(x_all)
    f.step()

    f["up_1"] = lines.out_1(f["up"])
    f["g_chip"], f["g_near"] = lines.to_chip(f["g_low"]), lines.over(f["g_low"])
    f["g_core"] = lines.to_core(f["g_low"])
    f["comb"] = unflat(mm(f["x_all"], f["w_mixer"]).astype(BF16))
    mixing = lambda: (f["order"], f["comb"], f["taps"], f["decay"], f["gain"])
    f["held"], f["links"] = mix_forward(0, 4, [], None, *mixing())
    f.step()

    f["up_2"] = lines.out_2(f["up_1"])
    f["g_both"] = [lines.to_chip(f["g_near"][0]), lines.over(f["g_chip"][1])]
    f["g_cores"] = lines.to_core(jnp.stack([f["g_chip"], f["g_near"]]))
    f["held"], f["links"] = mix_forward(4, 8, f["held"], f["links"], *mixing())
    f.step()

    up_3 = lines.out_3(f["up_2"])
    f["g_both"] = jnp.stack(f["g_both"])
    f["g_both_core"] = lines.to_core(f["g_both"])
    f["held"], f["links"] = mix_forward(12, 4, f["held"], f["links"], *mixing())

    to_out = lambda row: unflat(mm(flat(f["held"][0][NEAR * row : NEAR * row + NEAR]), mixer_out).astype(BF16))
    f["out_3"] = to_out(3)
    g_cores = f.take("g_cores")
    f["g_all"] = jnp.stack(
        [f.take("g_low"), f.take("g_core"), f.take("g_chip"), g_cores[0], f.take("g_near"), g_cores[1]]
    )
    f.step()

    f["got"] = lines.over(f["out_3"][1])
    f["out_2"], f["out_1"], f["out_0"] = to_out(2), to_out(1), to_out(0)
    f["up_3"] = up_3
    both = f.take("g_both", "g_both_core")
    f["g_all"] = flat(jnp.concatenate([f["g_all"], jnp.stack(both)]))
    f.step()

    f["sum_3"] = low_sum(f.take("out_3")[0], f.take("got"))
    f["got_3"] = lines.in_3(f["sum_3"])
    f["got"] = lines.over(f["out_2"][1])
    f["w_up"] = lines.line_whole(*f.take("up", "up_1", "up_2", "up_3")).reshape(width, 2 * half_ff)
    f["down_1"] = lines.out_1(f["down"])
    f.step()

    f["sum_2"] = low_sum(f.take("out_2")[0], f.take("got"))
    f["got_2"] = lines.in_2(f.take("sum_3"), f.take("got_3"), f["sum_2"])
    f["got"] = lines.over(f["out_1"][1])
    f.step()

    sum_1 = low_sum(f.take("out_1")[0], f.take("got"))
    f["got_1"] = lines.in_1(f.take("sum_2"), f.take("got_2"), sum_1)
    f["got"] = lines.over(f["out_0"][1])
    f.step()

    own = f.take("out_0")[0].astype(F32) + f.take("got").astype(F32)
    f["resid"] = resid = inputs.astype(F32) + lines.sum_0(own, f.take("got_1"))
    f["feed"] = (resid * rms_rate(resid)).astype(BF16)
    f.step()

    f["f_chip"], f["f_near"] = lines.to_chip(f["feed"]), lines.over(f["feed"])
    f["f_core"] = lines.to_core(f["feed"])
    f["down_2"] = lines.out_2(f["down_1"])
    f.step()

    f["f_both"] = [lines.to_chip(f["f_near"][0]), lines.over(f["f_chip"][1])]
    f["f_cores"] = lines.to_core(jnp.stack([f["f_chip"], f["f_near"]]))
    f["down_3"] = lines.out_3(f["down_2"])
    f.step()

    f["f_both"] = jnp.stack(f["f_both"])
    f["f_both_core"] = lines.to_core(f["f_both"])
    w_down = lines.line_whole(*f.take("down", "down_1", "down_2", "down_3")).reshape(2, 2 * cut, width)
    f["w_down"] = jnp.pad(w_down, ((0, 0), (0, group - 2 * cut), (0, 0))).reshape(half_ff, width)
    f.step()

    cores = f.take("f_cores")
    f["feed_all"] = flat(
        jnp.stack(
            [f.take("feed"), f.take("f_core"), f.take("f_chip"), cores[0], f.take("f_near"), cores[1]]
            + f.take("f_both", "f_both_core")
        )
    )
    pre = mm(f["feed_all"], f["w_up"]).astype(BF16)
    f["hidden"], f["g_pre"] = feed_forward(pre, mm_nt(f["g_all"], f["w_down"]))
    by_piece = lambda item: item.reshape(-1, piece, item.shape[1])
    to_feed = lambda *places: unflat(mm_nt(at(by_piece(f["g_pre"]), *places).reshape(-1, 2 * half_ff), f["w_up"]).astype(BF16))
    f["back_3"] = to_feed(6, 7)
    f.step()

    f["core_3"] = lines.to_core(f["back_3"][1])
    f["back_12"] = to_feed(2, 4, 3, 5)
    f.step()

    f["core_12"] = lines.to_core(f["back_12"][2:])
    sum_3 = low_sum(f.take("back_3")[0], f.take("core_3"))
    f["half_chip"], f["half_near"] = lines.to_chip(sum_3[0]), lines.over(sum_3[1])
    f["back_0"] = to_feed(0, 1)
    f.step()

    back, got = f.take("back_12", "core_12")
    half_chip, half_near = f.take("half_chip", "half_near")
    by_chip, by_near = low_sum(back[0], got[0]), low_sum(back[1], got[1])
    f["b_near"] = lines.over(jnp.stack([low_sum(by_near[0], half_chip), by_near[1]]))
    f["b_chip"] = lines.to_chip(jnp.stack([by_chip[0], low_sum(by_chip[1], half_near)]))
    f["core_0"] = lines.to_core(f["back_0"][1])
    f["out_part"] = mm(f["hidden"], f["w_down"]).astype(BF16).reshape(4, 2, slots, seg, width)
    f.step()

    g_feed = f.take("back_0")[0].astype(F32)
    for name in ("core_0", "b_chip", "b_near"):
        g_feed = g_feed + f.take(name).astype(F32)
    g_out = masked(out_cotangent, slot_length, lines.me)
    f["g_resid"] = g_resid = g_out + rms_back(f["resid"], rms_rate(f["resid"]), g_feed)
    f["r_low"] = g_resid.astype(BF16)
    f.step()

    f["r_1"] = lines.out_1(f["r_low"])
    f["over_0"] = lines.over(f["r_low"])
    f["up_term"] = mm_tn(f.take("feed_all"), f.take("g_pre")).astype(BF16).reshape(FAR, NEAR, rows, 2 * half_ff)
    f.step()

    f["line_1"] = lines.line_1(f["r_1"])
    f["over_1"] = lines.over(f["line_1"])
    f["r_2"] = lines.out_2(f["r_1"])
    down_term = mm_tn(f.take("hidden"), f.take("g_all")).reshape(2, group, width)[:, : 2 * cut]
    f["down_term"] = down_term.astype(BF16).reshape(FAR, cut, width)
    f["out_core"] = lines.to_core(f["out_part"][:, 1])
    f.step()

    f["line_2"] = lines.line_2(f.take("r_1"), f["r_2"])
    f["over_2"] = lines.over(f["line_2"])
    f["r_3"] = lines.out_3(f["r_2"])
    f["d_3"] = taken(f["down_term"], lines.rows[3])
    f["d_got_3"] = lines.in_3(f["d_3"])
    f["out_sum"] = low_sum(f.take("out_part")[:, 0], f.take("out_core"))
    f.step()

    f["line_3"] = lines.line_3(f.take("r_2"), f.take("r_3"))
    f["over_3"] = lines.over(f["line_3"])
    f["d_2"] = taken(f["down_term"], lines.rows[2])
    f["d_got_2"] = lines.in_2(f.take("d_3"), f.take("d_got_3"), f["d_2"])
    f["half_chip"] = lines.to_chip(f["out_sum"][3, 0])
    f.step()

    f["r_all"] = flat(
        jnp.stack(f.take("r_low", "over_0", "line_1", "over_1", "line_2", "over_2", "line_3", "over_3"))
    )
    f["g_head"] = unflat(mm_nt(f["r_all"], mixer_out).astype(BF16))
    f["half_near"] = lines.over(f["out_sum"][3, 1])
    head_term = mm_tn(flat(f["held"][0]), f.take("r_all")).astype(BF16).reshape(2, wide // 2, width)
    f["head_kept"], f["head_given"] = taken(head_term, lines.core), taken(head_term, 1 - lines.core)
    d_1 = taken(f["down_term"], lines.rows[1])
    f["d_got_1"] = lines.in_1(f.take("d_2"), f.take("d_got_2"), d_1)
    f["u_3"] = taken(f["up_term"], lines.rows[3])
    f.step()

    def backward(first, steps, held, links):
        held, terms, links = mix_backward(first, steps, held, links, *mixing(), f["held"][1:], f["g_head"])
        f["grads"], f["back_links"] = held, links
        f["terms"] = [a + b for a, b in zip(f["terms"], terms)] if first else terms

    f["u_got_3"] = lines.in_3(f["u_3"])
    out_sum, half_chip, half_near = f.take("out_sum", "half_chip", "half_near")
    f["own_out"] = out_sum[0]
    f["o_near"] = lines.over(jnp.stack([low_sum(out_sum[2, 0], half_chip), out_sum[2, 1]]))
    f["o_chip"] = lines.to_chip(jnp.stack([out_sum[1, 0], low_sum(out_sum[1, 1], half_near)]))
    f["head_got"] = lines.to_core(f.take("head_given"))
    backward(0, 5, [], None)
    f["down_sum"] = lines.sum_0(taken(f.take("down_term"), far), f.take("d_got_1")).astype(BF16)
    f.step()

    layer_out = f["resid"]
    for name in ("own_out", "o_near", "o_chip"):
        layer_out = layer_out + f.take(name).astype(F32)
    layer_out = layer_out.astype(BF16)
    f["u_2"] = taken(f["up_term"], lines.rows[2])
    f["u_got_2"] = lines.in_2(f.take("u_3"), f.take("u_got_3"), f["u_2"])
    f["head_half"] = low_sum(f.take("head_kept"), f.take("head_got"))
    f["head_chip"], f["down_core"] = lines.to_chip(f["head_half"]), lines.to_core(f["down_sum"])
    backward(5, 6, f["grads"], f["back_links"])
    f.step()

    f["u_got_1"] = lines.in_1(f.take("u_2"), f.take("u_got_2"), taken(f["up_term"], lines.rows[1]))
    f["head_half"] = low_sum(f["head_half"], f.take("head_chip"))
    f["head_core"], f["down_chip"] = lines.to_core(f["head_half"]), lines.to_chip(f["down_sum"])
    backward(11, 5, f["grads"], f["back_links"])
    f.step()

    early = 2 * wide
    f["g_mixer"] = f.take("grads")[0]
    f["down_both"] = lines.to_core(f["down_chip"])
    as_parts = lambda term: term.astype(BF16).reshape(FAR * NEAR, 2, 2, rows // copies, -1)
    f["a_term"] = as_parts(mm_tn(f["x_all"], flat(f["g_mixer"][..., :early])))
    f["up_sum"] = lines.sum_0(taken(f.take("up_term"), far), f.take("u_got_1")).astype(BF16)
    f["small"] = small.terms(*f.take("terms"))
    f["small_1"] = lines.to_core(f["small"])
    f.step()

    core_kept = lambda term: lax.dynamic_index_in_dim(term, lines.core, 2, keepdims=False)
    core_given = lambda term: lax.dynamic_index_in_dim(term, 1 - lines.core, 2, keepdims=False)
    f["a_kept"], f["a_got"] = core_kept(f["a_term"]), lines.to_core(core_given(f.take("a_term")))
    f["b_term"] = as_parts(mm_tn(f["x_all"], flat(f["g_mixer"][..., early:])))

    def pair(item, row):
        return lax.dynamic_slice_in_dim(item, row * NEAR, NEAR, 0).reshape(NEAR * piece, -1)

    kept, given = lambda pieces: taken(pieces, near), lambda pieces: taken(pieces, 1 - near)
    to_norm = lambda row: unflat(mm_nt(pair(f["g_mixer"], lines.rows[row]), f["w_mixer"]).astype(BF16))
    f["out_3"] = to_norm(3)
    f["up_over"] = lines.over(taken(f["up_sum"], 1 - near))
    f["small"] = f["small"] + f.take("small_1")
    f["small_1"] = lines.to_chip(f["small"])
    f.step()

    chip_kept = lambda term: lax.dynamic_index_in_dim(term, lines.chip, 1, keepdims=False)
    chip_given = lambda term: lax.dynamic_index_in_dim(term, 1 - lines.chip, 1, keepdims=False)
    half = low_sum(f.take("a_kept"), f.take("a_got"))
    f["a_half"], f["a_got"] = chip_kept(half), lines.to_chip(chip_given(half))
    f["b_kept"], f["b_got"] = core_kept(f["b_term"]), lines.to_core(core_given(f.take("b_term")))
    f["got"] = lines.over(given(f["out_3"]))
    f["out_2"], f["out_1"], f["out_0"] = to_norm(2), to_norm(1), to_norm(0)
    own, other = taken(f.take("up_sum"), near), f.take("up_over")
    f["up_own"] = jnp.where(near == 0, jnp.stack([own, other]), jnp.stack([other, own]))
    f["up_core"] = lines.to_core(f["up_own"])
    f["small"] = (f["small"] + f.take("small_1"))[None]
    f["small_1"] = lines.crossed(f["small"], 1)
    f.step()

    f["sum_3"] = low_sum(kept(f.take("out_3")), f.take("got"))
    f["got_3"] = lines.in_3(f["sum_3"])
    f["got"] = lines.over(given(f["out_2"]))
    half = low_sum(f.take("b_kept"), f.take("b_got"))
    f["b_half"], f["b_got"] = chip_kept(half), lines.to_chip(chip_given(half))
    f["a_own"] = lax.all_to_all(low_sum(f.take("a_half"), f.take("a_got")), "shard", 0, 0)
    f["small"] = jnp.concatenate([f["small"], f.take("small_1")])
    f["small_1"] = lines.crossed(f["small"], 2)
    f.step()

    f["sum_2"] = low_sum(kept(f.take("out_2")), f.take("got"))
    f["got_2"] = lines.in_2(f.take("sum_3"), f.take("got_3"), f["sum_2"])
    f["got"] = lines.over(given(f["out_1"]))
    f["up_chip"] = lines.to_chip(f["up_own"])
    f["b_own"] = lax.all_to_all(low_sum(f.take("b_half"), f.take("b_got")), "shard", 0, 0)
    f["small"] = jnp.concatenate([f["small"], f.take("small_1")])
    f["small_1"] = lines.crossed(f["small"], 4)
    f.step()

    sum_1 = low_sum(kept(f.take("out_1")), f.take("got"))
    f["got_1"] = lines.in_1(f.take("sum_2"), f.take("got_2"), sum_1)
    f["got"] = lines.over(given(f["out_0"]))
    f["up_both"] = lines.to_core(f["up_chip"])
    f["a_chip"] = lines.to_chip(f["a_own"])
    f.step()

    own = kept(f.take("out_0")).astype(F32) + f.take("got").astype(F32)
    g_norm = lines.sum_0(own, f.take("got_1"))
    xs = inputs.astype(F32)
    f["input_grad"] = (f.take("g_resid") + rms_back(xs, rms_rate(xs), g_norm)).astype(BF16)
    f["b_chip"] = lines.to_chip(f["b_own"])
    f["a_core"], f["b_core"], f["a_both"] = lines.to_core(f["a_own"]), lines.to_core(f["b_own"]), lines.to_core(f["a_chip"])
    ups = jnp.stack(f.take("up_own", "up_core", "up_chip", "up_both"))
    f["grad_up"], f["up_dots"] = merge_columns(copy, ups, gate_up, gain_feed, cut, group)
    grad_down = lines.quarters(*f.take("down_sum", "down_core", "down_chip", "down_both"))
    f["grad_down"] = grad_down.reshape(ff, width).astype(F32)
    f.step()

    a_all = jnp.stack(f.take("a_own", "a_core", "a_chip", "a_both"))
    head_half, head_core = f.take("head_half", "head_core")
    f["grad_out"] = jnp.where(
        lines.core == 0, jnp.concatenate([head_half, head_core]), jnp.concatenate([head_core, head_half])
    ).astype(F32)
    b_both = lines.to_core(f["b_chip"])
    b_all = jnp.stack(f.take("b_own", "b_core", "b_chip") + [b_both])
    g_in, g_gate, dots = unpack_mixer(copy, a_all, b_all, mixer_in, gate_weight, gain_in)
    quarters = jnp.take(b_all[..., 2 * small.narrow :], lax.iota(jnp.int32, copies) ^ lines.copy, axis=0)
    ab = jnp.moveaxis(quarters, 1, 2).reshape(rows, FAR * NEAR, DK).astype(F32)
    heads = small.heads
    ab = jnp.concatenate([ab[:, :, :heads].reshape(rows, -1), ab[:, :, heads : 2 * heads].reshape(rows, -1)], axis=1)
    g_norm = dots[:, 0] + jnp.sum(alpha_beta.astype(F32) * ab, axis=1)
    gathered = jnp.take(
        jnp.concatenate([f["small"], f["small_1"]]), lax.iota(jnp.int32, FAR * NEAR) ^ lines.me, axis=0
    )
    g_taps, g_gain, g_log, g_bias = small.gradients(gathered)
    return (
        layer_out, f["input_grad"], g_norm, g_in, g_gate, gain_in * ab, g_taps, g_log, g_bias, g_gain,
        f["grad_out"], f["up_dots"][:, 0], f["grad_up"], f["grad_down"],
    )


def solution(mesh):
    tokens, rows = P("rep", "shard", None), P("shard", None)
    return jax.shard_map(
        on_device,
        mesh=mesh,
        in_specs=(
            tokens, tokens, P("rep"), P("shard"), rows, rows, rows, P(None, "shard"), P(), P(),
            P("shard"), rows, P("shard"), rows, rows,
        ),
        out_specs=(
            tokens, tokens, P("shard"), rows, rows, rows, P(None, "shard"), P(), P(),
            P("shard"), rows, P("shard"), rows, rows,
        ),
        check_vma=False,
    )
```

```python
import functools
import jax
import jax.numpy as jnp
from jax import lax
from jax.experimental import pallas as pl
from jax.experimental.pallas import tpu as pltpu
from jax.sharding import PartitionSpec as P

DK = 128
DV = 256
CONV = 4
SPAN = 64
EPS = 1e-06
F32 = jnp.float32
BF16 = jnp.bfloat16
HIGH = lax.Precision.HIGHEST


def dot(left, right, dims, precision=None):
    return lax.dot_general(
        left, right, ((dims[0], dims[1]), ((), ())), precision=precision, preferred_element_type=F32
    )


def mm(left, right):
    return dot(left.astype(BF16), right.astype(BF16), ((1,), (0,)))


def mm_nt(left, right):
    return dot(left.astype(BF16), right.astype(BF16), ((1,), (1,)))


def mm_tn(left, right):
    return dot(left.astype(BF16), right.astype(BF16), ((0,), (0,)))


def softplus(v):
    return jnp.maximum(v, 0.0) + jnp.log(1.0 + jnp.exp(-jnp.abs(v)))


def sigmoid(v):
    return 1.0 / (1.0 + jnp.exp(-v))


def iotas(rows, cols):
    return (
        lax.broadcasted_iota(jnp.int32, (rows, cols), 0),
        lax.broadcasted_iota(jnp.int32, (rows, cols), 1),
    )


def unit_inverses(systems):
    if len(systems) % 2:
        pairs = [(m, m) for m in systems]
    else:
        pairs = [(systems[i], systems[i + 1]) for i in range(0, len(systems), 2)]
    rows, lanes = iotas(SPAN, 2 * SPAN)
    base = lanes - lax.rem(lanes, SPAN)
    packed = [jnp.concatenate(p, axis=1) for p in pairs]
    held = [jnp.where(rows == lax.rem(lanes, SPAN), 1.0, 0.0).astype(F32) for _ in pairs]
    for j in range(SPAN - 1):
        low = (j + 1) // 8 * 8
        for i in range(len(pairs)):
            col = jnp.take_along_axis(packed[i][low:], base[low:] + j, axis=1)
            new = held[i][low:] - col * held[i][j : j + 1]
            held[i] = jnp.concatenate([held[i][:low], new], axis=0) if low else new
    out = []
    for i in range(len(pairs)):
        out.append(held[i][:, :SPAN])
        if len(systems) % 2 == 0:
            out.append(held[i][:, SPAN:])
    return out


def gates(lg, dec_log, dec_bias):
    beta = sigmoid(lg)
    log_decay = -jnp.exp(dec_log) * softplus(lg + dec_bias)
    rows, cols = iotas(SPAN, SPAN)
    cumul = dot(jnp.where(rows >= cols, 1.0, 0.0).astype(F32), log_decay, ((1,), (0,)), HIGH)
    return beta, log_decay, cumul


def conv_act(ext, s, taps):
    total = taps[0:1] * ext[s, 5 : 5 + SPAN]
    for place in range(1, CONV):
        total = total + taps[place : place + 1] * ext[s, 5 + place : 5 + place + SPAN]
    return total


def unit_parts(act, h, heads):
    v = act[:, h * DV : (h + 1) * DV]
    a = act[:, heads * DV + h * DK : heads * DV + (h + 1) * DK]
    b = act[:, heads * (DV + DK) + h * DK : heads * (DV + DK) + (h + 1) * DK]
    qs = lax.rsqrt(jnp.sum(a * a, axis=-1, keepdims=True) + EPS)
    ks = lax.rsqrt(jnp.sum(b * b, axis=-1, keepdims=True) + EPS)
    return a, b, v, qs, ks


def decays(cumul, h, heads):
    col = cumul[:, heads + h : heads + h + 1]
    rows, cols = iotas(SPAN, SPAN)
    row = jnp.transpose(jnp.broadcast_to(col, (SPAN, SPAN)))
    spread = jnp.where(rows >= cols, jnp.broadcast_to(col, (SPAN, SPAN)) - row, 0.0)
    decay = jnp.where(rows >= cols, jnp.exp(spread), 0.0)
    growth = jnp.exp(col)
    last = col[SPAN - 1 : SPAN]
    tail = jnp.exp(last - col)
    return decay, growth, tail, jnp.exp(last), rows > cols


def fwd_body(heads, slots, held, order, comb, taps_ref, dec, hn, carry_in, state_in, *rest):
    head, mixed, t_out, s_out, u_out, carry, state, ext = rest[held:]

    @pl.when(pl.program_id(0) == 0)
    def _():
        carry[...] = carry_in[...]
        state[...] = state_in[...]

    gated, seen_by = heads * DV, heads * (2 * DV + 2 * DK)
    taps = taps_ref[...]
    units = []
    for s in range(slots):
        cur = comb[0, s, :, gated:seen_by].astype(F32)
        ext[s, 0:8] = carry[s]
        ext[s, 8 : 8 + SPAN] = cur
        carry[s] = cur[SPAN - 8 :]
        conv = conv_act(ext, s, taps)
        act = conv * sigmoid(conv)
        beta, unused, cumul = gates(comb[0, s, :, seen_by:].astype(F32), dec[0:1], dec[1:2])
        for h in range(heads):
            a, b, v, qs, ks = unit_parts(act, h, heads)
            q = (a * (qs * DK ** (-0.5))).astype(BF16)
            k32 = b * ks
            k = k32.astype(BF16)
            decay, growth, tail, last, strict = decays(cumul, h, heads)
            both = mm_nt(jnp.concatenate([q, k], axis=0), k)
            bcol = beta[:, h : h + 1]
            system = jnp.where(strict, bcol * decay * both[SPAN:], 0.0)
            scores = both[:SPAN] * decay
            units.append((s, h, q, k, k32, v, decay, growth, tail, last, bcol, system, scores))
    inverses = unit_inverses([u[11] for u in units])
    for i, (s, h, q, k, k32, v, decay, growth, tail, last, bcol, system, scores) in enumerate(units):
        inverse = inverses[i].astype(BF16)
        t_out[0, i] = inverse
        old = state[i]
        old_low = old.astype(BF16)
        s_out[0, i] = old_low
        seen = mm(jnp.concatenate([k, q], axis=0), old_low)
        target = bcol * (v - growth * seen[:SPAN])
        pseudo = mm(inverse, target).astype(BF16)
        u_out[0, i] = pseudo
        out = growth * seen[SPAN:] + mm(scores, pseudo)
        state[i] = last * old + mm_tn(k32 * tail, pseudo)
        mixed[0, s, :, h * DV : (h + 1) * DV] = out
        scale = lax.rsqrt(jnp.mean(out * out, axis=-1, keepdims=True) + EPS)
        pre = comb[0, s, :, h * DV : (h + 1) * DV].astype(F32)
        head[0, s, :, h * DV : (h + 1) * DV] = (out * scale * hn[0:1] * (pre * sigmoid(pre))).astype(BF16)


def bwd_body(
    heads, slots, left, held, order,
    comb, prev, taps_ref, dec, hn, mixed, t_in, s_in, u_in, g_head, carry_in, state_in, *rest,
):
    g_comb, g_taps, g_hn, g_dec, carry, state, ext, gext = rest[held:]
    gated, seen_by = heads * DV, heads * (2 * DV + 2 * DK)
    step = pl.program_id(0)

    @pl.when(step == 0)
    def _():
        carry[...] = carry_in[...]
        state[...] = state_in[...]
        g_taps[...] = jnp.zeros_like(g_taps)
        g_hn[...] = jnp.zeros_like(g_hn)
        g_dec[...] = jnp.zeros_like(g_dec)

    taps = taps_ref[...]
    inner = jnp.where(step == left - 1, 0.0, 1.0).astype(F32)
    rows, cols = iotas(SPAN, SPAN)
    lane = lax.broadcasted_iota(jnp.int32, (SPAN, DK), 1)
    trow = lax.broadcasted_iota(jnp.int32, (SPAN, 1), 0)
    for s in range(slots):
        cur = comb[0, s, :, gated:seen_by].astype(F32)
        logits = comb[0, s, :, seen_by:].astype(F32)
        ext[s, 0:8] = prev[0, s, SPAN - 8 :, gated:seen_by].astype(F32) * inner
        ext[s, 8 : 8 + SPAN] = cur
        conv = conv_act(ext, s, taps)
        sig = sigmoid(conv)
        act = conv * sig
        beta, log_decay, cumul = gates(logits, dec[0:1], dec[1:2])
        g_q, g_k, g_v = [], [], []
        d_beta = jnp.zeros((SPAN, DK), F32)
        d_cum = jnp.zeros((SPAN, DK), F32)
        for h in range(heads):
            i = s * heads + h
            a, b, v, qs, ks = unit_parts(act, h, heads)
            q32 = a * (qs * DK ** (-0.5))
            k32 = b * ks
            q, k = q32.astype(BF16), k32.astype(BF16)
            decay, growth, tail, last, strict = decays(cumul, h, heads)
            both = mm_nt(jnp.concatenate([q, k], axis=0), k)
            bcol = beta[:, h : h + 1]
            inverse, old, pseudo = t_in[0, i], s_in[0, i], u_in[0, i]
            scores = both[:SPAN] * decay
            span = slice(h * DV, (h + 1) * DV)
            go = g_head[0, s, :, span].astype(F32)
            pre = comb[0, s, :, span].astype(F32)
            sg = sigmoid(pre)
            out = mixed[0, s, :, span].astype(F32)
            scale = lax.rsqrt(jnp.mean(out * out, axis=-1, keepdims=True) + EPS)
            unit = out * scale
            g_comb[0, s, :, span] = (go * unit * hn[0:1] * (sg * (1.0 + pre * (1.0 - sg)))).astype(BF16)
            up = go * (pre * sg)
            g_hn[0:1] += jnp.sum(up * unit, axis=0, keepdims=True)
            e = up * hn[0:1]
            d_out = scale * (e - unit * jnp.mean(e * unit, axis=-1, keepdims=True))
            d_out_low = d_out.astype(BF16)
            d_next = state[i]
            d_next_low = d_next.astype(BF16)
            d_pseudo = mm_tn(scores, d_out_low) + mm(k32 * tail, d_next_low)
            d_right = mm_tn(inverse, d_pseudo)
            d_right_low = d_right.astype(BF16)
            both_g = jnp.concatenate([d_out_low, d_right_low], axis=0)
            state[i] = last * d_next + mm_tn(
                jnp.concatenate([growth * q32, -(growth * bcol) * k32], axis=0), both_g
            )
            by_state = mm_nt(both_g, old)
            by_pseudo = mm_nt(both_g, pseudo)
            out_state, right_state = by_state[:SPAN], by_state[SPAN:]
            tail_state = mm_nt(pseudo, d_next_low)
            d_scores = by_pseudo[:SPAN]
            d_system = jnp.where(strict, -by_pseudo[SPAN:], 0.0)
            d_att = d_scores * decay
            d_inter = d_system * decay
            square = d_att * both[:SPAN] + d_inter * both[SPAN:] * bcol
            pair = jnp.concatenate([d_att, d_inter * bcol], axis=0)
            first = mm(pair, k)
            second = mm_tn(pair, jnp.concatenate([q, k], axis=0))
            out_q = growth * jnp.sum(out_state * q32, axis=-1, keepdims=True)
            right_k = growth * jnp.sum(right_state * k32, axis=-1, keepdims=True)
            tail_k = tail * jnp.sum(tail_state * k32, axis=-1, keepdims=True)
            dq = growth * out_state + first[:SPAN]
            dk = first[SPAN:] + second - (growth * bcol) * right_state + tail * tail_state
            dv = bcol * d_right
            db = (
                jnp.sum(d_right * v, axis=-1, keepdims=True)
                - right_k
                + jnp.sum(d_inter * both[SPAN:], axis=-1, keepdims=True)
            )
            dc = (
                jnp.sum(square - jnp.transpose(square), axis=-1, keepdims=True)
                + out_q
                - bcol * right_k
                - tail_k
            )
            at_last = jnp.sum(tail_k, axis=0, keepdims=True) + last * jnp.sum(
                jnp.sum(d_next * old.astype(F32), axis=-1, keepdims=True), axis=0, keepdims=True
            )
            dc = dc + jnp.where(trow == SPAN - 1, at_last, 0.0)
            d_beta = jnp.where(lane == h, db, d_beta)
            d_cum = jnp.where(lane == heads + h, dc, d_cum)
            qh = a * qs
            g_q.append((qs * DK ** (-0.5)) * (dq - qh * jnp.sum(qh * dq, axis=-1, keepdims=True)))
            g_k.append(ks * (dk - k32 * jnp.sum(k32 * dk, axis=-1, keepdims=True)))
            g_v.append(dv)
        d_log = dot(jnp.where(cols >= rows, 1.0, 0.0).astype(F32), d_cum, ((1,), (0,)), HIGH)
        pre_gate = logits + dec[1:2]
        d_alpha = d_log * (-jnp.exp(dec[0:1])) * sigmoid(pre_gate)
        g_dec[0:1] += jnp.sum(d_log * log_decay, axis=0, keepdims=True)
        g_dec[1:2] += jnp.sum(d_alpha, axis=0, keepdims=True)
        g_comb[0, s, :, seen_by:] = (d_beta * beta * (1.0 - beta) + d_alpha).astype(BF16)
        g_act = jnp.concatenate(g_v + g_q + g_k, axis=1)
        g_conv = g_act * (sig * (1.0 + conv * (1.0 - sig)))
        gext[s, 0:SPAN] = g_conv
        gext[s, SPAN : SPAN + 8] = carry[s]
        carry[s] = g_conv[0:8]
        total = taps[CONV - 1 : CONV] * g_conv
        for place in range(CONV):
            g_taps[place : place + 1] += jnp.sum(
                g_conv * ext[s, 5 + place : 5 + place + SPAN], axis=0, keepdims=True
            )
            if place < CONV - 1:
                total = total + taps[place : place + 1] * gext[s, CONV - 1 - place : CONV - 1 - place + SPAN]
        g_comb[0, s, :, gated:seen_by] = total.astype(BF16)


def geometry(comb):
    shards, slots, seg, wide = comb.shape
    heads = (wide - DK) // (2 * DK + 2 * DV)
    return shards, slots, seg, heads, seg // SPAN, wide


def token_spec(slots, width, per, at):
    return pl.BlockSpec(
        (1, slots, SPAN, width), lambda n, order: (order[at(n) // per], 0, lax.rem(at(n), per), 0)
    )


def fixed_spec(*shape):
    return pl.BlockSpec(shape, lambda n, order: (0,) * len(shape))


def no_links(slots, heads):
    return [jnp.zeros((slots, 8, heads * (2 * DK + DV)), F32), jnp.zeros((slots * heads, DK, DV), F32)]


def mix_forward(first, steps, held, links, order, comb, taps, dec, hn):
    shards, slots, seg, heads, per, wide = geometry(comb)
    spans, chains, chans = shards * per, slots * heads, heads * (2 * DK + DV)
    at = lambda n: n + first
    tok = lambda width: token_spec(slots, width, per, at)
    unit = lambda *shape: pl.BlockSpec((1, chains) + shape, lambda n, order: (at(n), 0, 0, 0))
    links = links or no_links(slots, heads)
    done = pl.pallas_call(
        functools.partial(fwd_body, heads, slots, len(held)),
        grid_spec=pltpu.PrefetchScalarGridSpec(
            num_scalar_prefetch=1,
            grid=(steps,),
            in_specs=[tok(wide)]
            + [fixed_spec(*a.shape) for a in (taps, dec, hn, *links)]
            + [pl.BlockSpec(memory_space=pl.ANY)] * len(held),
            out_specs=[
                token_spec(slots, heads * DV, per, at), tok(heads * DV),
                unit(SPAN, SPAN), unit(DK, DV), unit(SPAN, DV),
                fixed_spec(slots, 8, chans), fixed_spec(chains, DK, DV),
            ],
            scratch_shapes=[pltpu.VMEM((slots, SPAN + 8, chans), F32)],
        ),
        out_shape=[
            jax.ShapeDtypeStruct((shards, slots, seg, heads * DV), BF16),
            jax.ShapeDtypeStruct((shards, slots, seg, heads * DV), F32),
            jax.ShapeDtypeStruct((spans, chains, SPAN, SPAN), BF16),
            jax.ShapeDtypeStruct((spans, chains, DK, DV), BF16),
            jax.ShapeDtypeStruct((spans, chains, SPAN, DV), BF16),
            jax.ShapeDtypeStruct((slots, 8, chans), F32),
            jax.ShapeDtypeStruct((chains, DK, DV), F32),
        ],
        input_output_aliases={7 + i: i for i in range(len(held))},
        compiler_params=pltpu.CompilerParams(vmem_limit_bytes=40 << 20),
        cost_estimate=pl.CostEstimate(
            flops=steps * chains * 600_000_000, bytes_accessed=steps * chains * 400_000, transcendentals=0
        ),
        name="mix_forward",
    )(order, comb, taps, dec, hn, *links, *held)
    return list(done[:5]), list(done[5:])


def mix_backward(first, steps, held, links, order, comb, taps, dec, hn, saved, g_head):
    shards, slots, seg, heads, per, wide = geometry(comb)
    spans, chains, chans = shards * per, slots * heads, heads * (2 * DK + DV)
    last = spans - 1 - first
    back = lambda n: last - n
    tok = lambda width: token_spec(slots, width, per, back)
    before = token_spec(slots, wide, per, lambda n: jnp.maximum(last - 1 - n, 0))
    unit = lambda *shape: pl.BlockSpec((1, chains) + shape, lambda n, order: (back(n), 0, 0, 0))
    links = links or no_links(slots, heads)
    done = pl.pallas_call(
        functools.partial(bwd_body, heads, slots, last + 1, len(held)),
        grid_spec=pltpu.PrefetchScalarGridSpec(
            num_scalar_prefetch=1,
            grid=(steps,),
            in_specs=[tok(wide), before]
            + [fixed_spec(*a.shape) for a in (taps, dec, hn)]
            + [tok(heads * DV), unit(SPAN, SPAN), unit(DK, DV), unit(SPAN, DV)]
            + [token_spec(slots, heads * DV, per, back)]
            + [fixed_spec(*a.shape) for a in links]
            + [pl.BlockSpec(memory_space=pl.ANY)] * len(held),
            out_specs=[
                tok(wide), fixed_spec(8, chans), fixed_spec(8, DV), fixed_spec(8, DK),
                fixed_spec(slots, 8, chans), fixed_spec(chains, DK, DV),
            ],
            scratch_shapes=[
                pltpu.VMEM((slots, SPAN + 8, chans), F32),
                pltpu.VMEM((slots, SPAN + 8, chans), F32),
            ],
        ),
        out_shape=[
            jax.ShapeDtypeStruct(comb.shape, BF16),
            jax.ShapeDtypeStruct((8, chans), F32),
            jax.ShapeDtypeStruct((8, DV), F32),
            jax.ShapeDtypeStruct((8, DK), F32),
            jax.ShapeDtypeStruct((slots, 8, chans), F32),
            jax.ShapeDtypeStruct((chains, DK, DV), F32),
        ],
        input_output_aliases={13 + i: i for i in range(len(held))},
        compiler_params=pltpu.CompilerParams(vmem_limit_bytes=40 << 20),
        cost_estimate=pl.CostEstimate(
            flops=steps * chains * 900_000_000, bytes_accessed=steps * chains * 600_000, transcendentals=0
        ),
        name="mix_backward",
    )(order, comb, comb, taps, dec, hn, *saved, g_head, *links, *held)
    return list(done[:1]), list(done[1:4]), list(done[4:])


HEADS = 16
FAR, NEAR = 4, 2
COPIES = 4
EXTRA, WIDTH = 64, 32


def taken(items, index):
    return lax.dynamic_index_in_dim(items, index, 0, keepdims=False)


def placed_at(items, item, index):
    return lax.dynamic_update_slice_in_dim(items, item[None], index, 0)


def low_sum(*terms):
    total = terms[0].astype(F32)
    for term in terms[1:]:
        total = total + term.astype(F32)
    return total.astype(BF16)


def after(item, *others):
    return lax.optimization_barrier((item,) + others)[0]


class Flow:
    def step(self):
        held = vars(self)
        leaves, tree = jax.tree.flatten(list(held.values()))
        held.update(zip(list(held), jax.tree.unflatten(tree, lax.optimization_barrier(tuple(leaves)))))

    def take(self, *items):
        for item in items:
            for name in [name for name, value in vars(self).items() if value is item]:
                delattr(self, name)
        return items[0] if len(items) == 1 else list(items)


def split_columns(step_rows, cut, gain, starts, weight, out):
    group = out.shape[2] // 4
    window = group + 128
    lanes = lax.broadcasted_iota(jnp.int32, (step_rows, group), 1)
    for side in range(2):
        for place in range(4):
            total = jnp.zeros((step_rows, group), F32)
            for half in range(2):
                start = starts[side, 2 * place + half]
                low = jnp.minimum(start // 128 * 128, weight.shape[1] - window)
                seen = weight[:, pl.ds(pl.multiple_of(low, 128), window)].astype(F32)
                shift = lax.rem(half * cut - (start - low) + window, window)
                moved = pltpu.roll(seen, shift, 1)[:, :group]
                keep = (lanes >= half * cut) & (lanes < (half + 1) * cut)
                total = jnp.where(keep, moved, total)
            out[side, :, place * group : (place + 1) * group] = (total * gain[...]).astype(BF16)


def pick_columns(weight, gain, starts, cut, group):
    rows, step = weight.shape[0], 64
    return pl.pallas_call(
        lambda starts, weight, gain, out: split_columns(step, cut, gain, starts, weight, out),
        grid_spec=pltpu.PrefetchScalarGridSpec(
            num_scalar_prefetch=1,
            grid=(rows // step,),
            in_specs=[
                pl.BlockSpec((step, weight.shape[1]), lambda n, starts: (n, 0)),
                pl.BlockSpec((step, 1), lambda n, starts: (n, 0)),
            ],
            out_specs=pl.BlockSpec((2, step, 4 * group), lambda n, starts: (0, n, 0)),
        ),
        out_shape=jax.ShapeDtypeStruct((2, rows, 4 * group), BF16),
        compiler_params=pltpu.CompilerParams(vmem_limit_bytes=40 << 20),
        name="pick_columns",
    )(starts, weight, gain)


def merge_body(cut, group, copy, parts, weight, gain, grad, dots):
    total = 0.0
    span = NEAR * COPIES * cut
    for which in range(2):
        for far in range(FAR):
            at = which * 2 * group + far // 2 * group + far % 2 * cut
            pieces = [
                parts[index ^ copy[0], near, :, at : at + cut].astype(F32)
                for near in range(NEAR)
                for index in range(COPIES)
            ]
            joined = jnp.concatenate(pieces, axis=1)
            here = pl.ds((which * FAR + far) * span, span)
            grad[:, here] = joined * gain[...]
            total = total + jnp.sum(weight[:, here].astype(F32) * joined, axis=1, keepdims=True)
    dots[...] = jnp.broadcast_to(total, dots.shape)


def merge_columns(copy, parts, weight, gain, cut, group):
    rows, cols, step = weight.shape[0], weight.shape[1], 32
    return pl.pallas_call(
        functools.partial(merge_body, cut, group),
        grid_spec=pltpu.PrefetchScalarGridSpec(
            num_scalar_prefetch=1,
            grid=(rows // step,),
            in_specs=[
                pl.BlockSpec((COPIES, NEAR, step, parts.shape[3]), lambda n, copy: (0, 0, n, 0)),
                pl.BlockSpec((step, cols), lambda n, copy: (n, 0)),
                pl.BlockSpec((step, 1), lambda n, copy: (n, 0)),
            ],
            out_specs=[
                pl.BlockSpec((step, cols), lambda n, copy: (n, 0)),
                pl.BlockSpec((step, 128), lambda n, copy: (n, 0)),
            ],
        ),
        out_shape=[jax.ShapeDtypeStruct((rows, cols), F32), jax.ShapeDtypeStruct((rows, 128), F32)],
        compiler_params=pltpu.CompilerParams(vmem_limit_bytes=40 << 20),
        name="merge_columns",
    )(copy, parts, weight, gain)


def pack_body(heads, copy, gate, value, query, key, ab, gain, out):
    device = pl.program_id(0)
    scaled = lambda weight: (weight[...].astype(F32) * gain[...]).astype(BF16)
    wide, narrow = heads * DV, heads * DK
    out[0, :, :wide] = scaled(gate)
    out[0, :, wide : 2 * wide] = scaled(value)
    out[0, :, 2 * wide : 2 * wide + narrow] = scaled(query)
    out[0, :, 2 * wide + narrow : 2 * wide + 2 * narrow] = scaled(key)
    both = ab[...].astype(F32) * gain[...]
    lanes = lax.broadcasted_iota(jnp.int32, both.shape, 1)
    strength = pltpu.roll(both, lax.rem(DK - heads * device, DK), 1)
    decay = pltpu.roll(both, lax.rem(DK + heads - HEADS - heads * device, DK), 1)
    extra = jnp.where((lanes >= EXTRA) & (lanes < EXTRA + WIDTH), ab[...].astype(F32), 0.0)
    out[0, :, 2 * wide + 2 * narrow :] = jnp.where(
        lanes < heads, strength, jnp.where(lanes < 2 * heads, decay, extra)
    ).astype(BF16)


def as_extra(vector, rows):
    return jnp.pad(vector, (0, rows * WIDTH - vector.shape[0])).reshape(rows, WIDTH)


def pack_mixer(copy, mixer_in, gate_weight, alpha_beta, gain, extra):
    devices = FAR * NEAR
    heads, rows = HEADS // devices, mixer_in.shape[0] // COPIES
    wide, narrow = heads * DV, heads * DK
    total = 2 * wide + 2 * narrow + DK
    ab = jnp.pad(alpha_beta, ((0, 0), (0, EXTRA - 2 * HEADS)))
    ab = jnp.concatenate([ab, jnp.pad(extra, ((0, 0), (0, DK - EXTRA - WIDTH)))], axis=1)
    return pl.pallas_call(
        functools.partial(pack_body, heads),
        grid_spec=pltpu.PrefetchScalarGridSpec(
            num_scalar_prefetch=1,
            grid=(devices,),
            in_specs=[
                pl.BlockSpec((rows, wide), lambda d, copy: (copy[0], d)),
                pl.BlockSpec((rows, wide), lambda d, copy: (copy[0], devices + d)),
                pl.BlockSpec((rows, narrow), lambda d, copy: (copy[0], d)),
                pl.BlockSpec((rows, narrow), lambda d, copy: (copy[0], devices + d)),
                pl.BlockSpec((rows, DK), lambda d, copy: (copy[0], 0)),
                pl.BlockSpec((rows, 1), lambda d, copy: (copy[0], 0)),
            ],
            out_specs=pl.BlockSpec((1, rows, total), lambda d, copy: (d, 0, 0)),
        ),
        out_shape=jax.ShapeDtypeStruct((devices, rows, total), BF16),
        compiler_params=pltpu.CompilerParams(vmem_limit_bytes=40 << 20),
        name="pack_mixer",
    )(copy, gate_weight, mixer_in, mixer_in, mixer_in, ab, gain)


def put_rows(copy, parts, weight, gain, out, dots, lanes):
    size = parts[0].shape[2]
    for index in range(COPIES):
        here = pl.ds(pl.multiple_of((index ^ copy[0]) * size, size), size)
        grad = parts[index][0].astype(F32)
        grad = jnp.concatenate([grad[which] for which in range(grad.shape[0])], axis=1)
        out[here, :] = grad[:, :lanes] * gain[here, :]
        total = jnp.sum(weight[here, :].astype(F32) * grad[:, :lanes], axis=1, keepdims=True)
        dots[here, :] += jnp.broadcast_to(total, (size, dots.shape[1]))


def wide_body(devices, copy, a, b, c, d, w_in, w_gate, gain, g_in, g_gate, dots):
    step = pl.program_id(0)

    @pl.when(step == 0)
    def _():
        dots[...] = jnp.zeros_like(dots)

    @pl.when(step < devices)
    def _():
        put_rows(copy, (a, b, c, d), w_in, gain, g_in, dots, w_in.shape[1])

    @pl.when(step >= devices)
    def _():
        put_rows(copy, (a, b, c, d), w_gate, gain, g_gate, dots, w_gate.shape[1])


def unpack_wide(copy, parts, mixer_in, gate_weight, gain):
    devices, rows = FAR * NEAR, mixer_in.shape[0]
    wide, quarter = HEADS // devices * DV, rows // COPIES
    into = lambda n, copy: (0, devices + jnp.minimum(n, devices - 1))
    gates = lambda n, copy: (0, jnp.maximum(n - devices, 0))
    part = pl.BlockSpec(
        (1, 1, quarter, wide), lambda n, copy: (0, lax.rem(n, devices), 0, 1 - n // devices)
    )
    parts = [item[None] for item in parts]
    return pl.pallas_call(
        functools.partial(wide_body, devices),
        grid_spec=pltpu.PrefetchScalarGridSpec(
            num_scalar_prefetch=1,
            grid=(2 * devices,),
            in_specs=[part] * COPIES
            + [
                pl.BlockSpec((rows, wide), into),
                pl.BlockSpec((rows, wide), gates),
                pl.BlockSpec((rows, 1), lambda n, copy: (0, 0)),
            ],
            out_specs=[
                pl.BlockSpec((rows, wide), into),
                pl.BlockSpec((rows, wide), gates),
                pl.BlockSpec((rows, 128), lambda n, copy: (0, 0)),
            ],
        ),
        out_shape=[
            jax.ShapeDtypeStruct(mixer_in.shape, F32),
            jax.ShapeDtypeStruct(gate_weight.shape, F32),
            jax.ShapeDtypeStruct((rows, 128), F32),
        ],
        compiler_params=pltpu.CompilerParams(vmem_limit_bytes=40 << 20),
        name="unpack_wide",
    )(copy, *parts, mixer_in, gate_weight, gain)


def narrow_body(heads, copy, a, b, c, d, e_a, e_b, e_c, e_d, w_in, w_ab, gain, begun, g_in, g_ab, dots):
    step = pl.program_id(0)

    @pl.when(step == 0)
    def _():
        dots[...] = jnp.zeros_like(dots)
        total = jnp.zeros(w_ab.shape, F32)
        size = e_a.shape[2]
        lanes = lax.broadcasted_iota(jnp.int32, (size, w_ab.shape[1]), 1)
        for index, part in enumerate((e_a, e_b, e_c, e_d)):
            here = pl.ds(pl.multiple_of((index ^ copy[0]) * size, size), size)
            grad = jnp.zeros((size, w_ab.shape[1]), F32)
            for device in range(part.shape[1]):
                item = part[0, device].astype(F32)
                low = pltpu.roll(item, device * heads, 1)
                high = pltpu.roll(item, HEADS + (device - 1) * heads, 1)
                grad = jnp.where((lanes >= device * heads) & (lanes < (device + 1) * heads), low, grad)
                at = HEADS + device * heads
                grad = jnp.where((lanes >= at) & (lanes < at + heads), high, grad)
            g_ab[here, :] = grad * gain[here, :]
            dot = jnp.sum(w_ab[here, :].astype(F32) * grad, axis=1, keepdims=True)
            dots[here, :] += jnp.broadcast_to(dot, (size, dots.shape[1]))

    put_rows(copy, (a, b, c, d), w_in, gain, g_in, dots, w_in.shape[1])


def unpack_narrow(copy, parts, mixer_in, alpha_beta, gain, begun):
    devices, rows = FAR * NEAR, mixer_in.shape[0]
    heads = HEADS // devices
    narrow, quarter = heads * DK, rows // COPIES
    ab = jnp.pad(alpha_beta, ((0, 0), (0, DK - 2 * HEADS)))
    pairs, before = devices // 2, 2 * heads * DV // narrow
    part = pl.BlockSpec((1, 2, quarter, narrow), lambda n, copy: (0, lax.rem(n, pairs), 0, before + n // pairs))
    extra = pl.BlockSpec((1, devices, quarter, DK), lambda n, copy: (0, 0, 0, (2 * heads * DV + 2 * narrow) // DK))
    fixed = lambda *shape: pl.BlockSpec(shape, lambda n, copy: (0, 0))
    into = pl.BlockSpec((rows, 2 * narrow), lambda n, copy: (0, n))
    parts = [item[None] for item in parts]
    g_in, g_ab, dots = pl.pallas_call(
        functools.partial(narrow_body, heads),
        grid_spec=pltpu.PrefetchScalarGridSpec(
            num_scalar_prefetch=1,
            grid=(devices,),
            in_specs=[part] * COPIES
            + [extra] * COPIES
            + [into, fixed(rows, DK), fixed(rows, 1), pl.BlockSpec(memory_space=pl.ANY)],
            out_specs=[into, fixed(rows, DK), fixed(rows, 128)],
        ),
        out_shape=[
            jax.ShapeDtypeStruct(mixer_in.shape, F32),
            jax.ShapeDtypeStruct((rows, DK), F32),
            jax.ShapeDtypeStruct((rows, 128), F32),
        ],
        input_output_aliases={2 * COPIES + 4: 0},
        compiler_params=pltpu.CompilerParams(vmem_limit_bytes=40 << 20),
        name="unpack_narrow",
    )(copy, *parts, *parts, mixer_in, ab, gain, begun)
    return g_in, g_ab[:, : 2 * HEADS], dots


def spread_body(me, *refs):
    out = refs[-1]
    for index, part in enumerate(refs[:-1]):

        @pl.when(pl.program_id(0) == index)
        def _(part=part):
            out[...] = part[...].astype(F32)


def spread(me, parts):
    rows, cols = parts[0].shape
    return pl.pallas_call(
        spread_body,
        grid_spec=pltpu.PrefetchScalarGridSpec(
            num_scalar_prefetch=1,
            grid=(len(parts),),
            in_specs=[pl.BlockSpec((rows, cols), lambda n, me: (0, 0))] * len(parts),
            out_specs=pl.BlockSpec((rows, cols), lambda n, me: (n ^ me[0], 0)),
        ),
        out_shape=jax.ShapeDtypeStruct((rows * len(parts), cols), F32),
        compiler_params=pltpu.CompilerParams(vmem_limit_bytes=40 << 20),
        name="spread",
    )(me.astype(jnp.int32)[None], *parts)


class Lines:
    def __init__(self):
        self.count, self.copies = lax.axis_size("shard"), lax.axis_size("rep")
        self.me, self.copy = lax.axis_index("shard"), lax.axis_index("rep")
        self.known = self.count == FAR * NEAR and self.copies == COPIES
        far = self.far = self.me // NEAR
        self.near = lax.rem(self.me, NEAR)
        self.chip, self.core = self.copy // 2, lax.rem(self.copy, 2)
        self.rows = (
            far,
            jnp.where(far == 0, 1, far - 1),
            jnp.where(far == 0, 2, jnp.where(far == 3, 1, far + 1)),
            jnp.where(far < 2, 3, 0),
        )

    def along(self, item, sources, by):
        return lax.ppermute(
            item, "shard", [(2 * z + y, 2 * (z + by) + y) for z in sources for y in range(2)]
        )

    def turned(self, item, by):
        return lax.ppermute(
            item, "shard", [(2 * z + y, 2 * ((z + by) % FAR) + y) for z in range(FAR) for y in range(2)]
        )

    def over(self, item):
        return lax.ppermute(item, "shard", [(i, i ^ 1) for i in range(FAR * NEAR)])

    def crossed(self, item, bit):
        return lax.ppermute(item, "shard", [(i, i ^ bit) for i in range(FAR * NEAR)])

    def to_core(self, item):
        return lax.ppermute(item, "rep", [(i, i ^ 1) for i in range(COPIES)])

    def to_chip(self, item):
        return lax.ppermute(item, "rep", [(i, i ^ 2) for i in range(COPIES)])

    def order(self):
        device = lax.iota(jnp.int32, FAR * NEAR)
        row, place = device // NEAR, jnp.zeros((FAR * NEAR,), jnp.int32)
        for index in range(1, FAR):
            place = jnp.where(row == self.rows[index], index, place)
        return (NEAR * place + (lax.rem(device, NEAR) ^ self.near)).astype(jnp.int32)

    def out_1(self, piece):
        return self.along(piece, (0, 1, 2), 1), self.along(piece, (1, 2, 3), -1)

    def out_2(self, got_1):
        return self.along(got_1[0], (1, 2), 1), self.along(got_1[1], (2, 1), -1)

    def ends(self, item, outward):
        pairs = [(1, 0), (2, 3)] if outward else [(0, 1), (3, 2)]
        return lax.ppermute(item, "shard", [(2 * a + y, 2 * b + y) for a, b in pairs for y in range(2)])

    def out_3(self, got_2):
        return self.ends(jnp.where(self.far == 1, got_2[1], got_2[0]), True)

    def line_1(self, got_1):
        return jnp.where(self.far == 0, got_1[1], got_1[0])

    def line_2(self, got_1, got_2):
        return jnp.where(self.far == 0, got_2[1], jnp.where(self.far == 3, got_2[0], got_1[1]))

    def line_3(self, got_2, got_3):
        far = self.far
        return jnp.where(far == 1, got_2[1], jnp.where(far == 2, got_2[0], got_3))

    def line_whole(self, piece, got_1, got_2, got_3):
        pieces = (piece, self.line_1(got_1), self.line_2(got_1, got_2), self.line_3(got_2, got_3))
        whole = jnp.zeros((FAR,) + piece.shape, piece.dtype)
        for row, item in zip(self.rows, pieces):
            whole = placed_at(whole, item, row)
        return whole

    def in_3(self, sum_3):
        return self.ends(sum_3, False)

    def in_2(self, sum_3, got_3, sum_2):
        passed = low_sum(sum_3, got_3)
        up = jnp.where(self.far == 3, sum_2, passed)
        down = jnp.where(self.far == 0, sum_2, passed)
        return self.along(up, (3, 2), -1), self.along(down, (0, 1), 1)

    def in_1(self, sum_2, got_2, sum_1):
        down = jnp.where(self.far == 0, sum_1, low_sum(sum_2, got_2[1]))
        return self.along(low_sum(sum_1, got_2[0]), (3, 2, 1), -1), self.along(down, (0, 1, 2), 1)

    def sum_0(self, own, got_1):
        return own.astype(F32) + got_1[0].astype(F32) + got_1[1].astype(F32)

    def own_quarter(self, rows):
        size = rows.shape[0] // self.copies
        return lax.dynamic_slice_in_dim(rows, self.copy * size, size, 0)

    def quarters(self, own, by_core, by_chip, by_both):
        chip, core = self.chip, self.core
        whole = jnp.zeros((COPIES,) + own.shape, own.dtype)
        whole = placed_at(whole, own, 2 * chip + core)
        whole = placed_at(whole, by_core, 2 * chip + 1 - core)
        whole = placed_at(whole, by_chip, 2 * (1 - chip) + core)
        return placed_at(whole, by_both, 2 * (1 - chip) + 1 - core)


def rms_back(values, scale, grad):
    mean = jnp.mean(grad * values, axis=-1, keepdims=True)
    return scale * grad - values * (scale * scale * scale) * mean


def rms_rate(values):
    return lax.rsqrt(jnp.mean(values * values, axis=-1, keepdims=True) + EPS)


class Small:
    def __init__(self, lines, conv_taps, head_norm):
        self.shards, self.me = lines.count, lines.me
        self.heads = HEADS // self.shards
        self.chan_part, self.gain_part = conv_taps.shape[1], head_norm.shape[0]
        self.narrow, self.wide = self.heads * DK, self.heads * DV
        self.chans = 2 * self.narrow + self.wide

    def parameters(self, gathered):
        taps = gathered[:, : CONV * self.chan_part].reshape(self.shards, CONV, self.chan_part)
        taps = jnp.moveaxis(taps, 0, 1).reshape(CONV, self.shards * self.chan_part)
        gain = jnp.broadcast_to(gathered[:, CONV * self.chan_part :].reshape(1, DV), (8, DV))
        key_width, first = HEADS * DK, self.me * self.heads
        taps = jnp.concatenate(
            [
                lax.dynamic_slice_in_dim(taps, 2 * key_width + first * DV, self.wide, 1),
                lax.dynamic_slice_in_dim(taps, first * DK, self.narrow, 1),
                lax.dynamic_slice_in_dim(taps, key_width + first * DK, self.narrow, 1),
            ],
            axis=1,
        )
        return jnp.pad(taps, ((0, 8 - CONV), (0, 0))), gain

    def decay(self, decay_log, decay_bias):
        def own(item):
            item = lax.dynamic_slice_in_dim(item, self.me * self.heads, self.heads, 0)
            return jnp.pad(item, (self.heads, DK - 2 * self.heads))

        return jnp.pad(jnp.stack([own(decay_log), own(decay_bias)]), ((0, 6), (0, 0)))

    def terms(self, g_taps, g_gain, g_decay):
        alpha = slice(self.heads, 2 * self.heads)
        return jnp.concatenate([g_taps[:CONV].reshape(-1), g_gain[0], g_decay[0, alpha], g_decay[1, alpha]])

    def gradients(self, gathered):
        end = CONV * self.chans
        taps = gathered[:, :end].reshape(self.shards, CONV, self.chans)
        taps = jnp.concatenate(
            [
                jnp.moveaxis(item, 0, 1).reshape(CONV, -1)
                for item in (
                    taps[:, :, self.wide : self.wide + self.narrow],
                    taps[:, :, self.wide + self.narrow :],
                    taps[:, :, : self.wide],
                )
            ],
            axis=1,
        )
        taps = lax.dynamic_slice_in_dim(taps, self.me * self.chan_part, self.chan_part, 1)
        gain = jnp.sum(gathered[:, end : end + DV], axis=0)
        gain = lax.dynamic_slice_in_dim(gain, self.me * self.gain_part, self.gain_part, 0)
        at = end + DV
        return taps, gain, gathered[:, at : at + self.heads].reshape(-1), gathered[:, at + self.heads :].reshape(-1)


def fanned(weight, shards):
    return jnp.moveaxis(weight.reshape(weight.shape[0], shards, -1), 1, 0)


def mixer_parts(mixer_rows, gate_rows, ab_rows, shards):
    key_width, heads = HEADS * DK, HEADS // shards
    ab = jnp.concatenate([fanned(ab_rows[:, :HEADS], shards), fanned(ab_rows[:, HEADS:], shards)], axis=2)
    return jnp.concatenate(
        [
            fanned(gate_rows, shards),
            fanned(mixer_rows[:, 2 * key_width :], shards),
            fanned(mixer_rows[:, :key_width], shards),
            fanned(mixer_rows[:, key_width : 2 * key_width], shards),
            jnp.pad(ab, ((0, 0), (0, 0), (0, DK - 2 * heads))),
        ],
        axis=2,
    )


def mixer_grads(small, owned, mixer_norm, mixer_in, gate_weight, alpha_beta):
    rows, heads = mixer_in.shape[0], small.heads
    gain = mixer_norm.astype(F32)[:, None]

    def joined(low, high):
        return jnp.moveaxis(owned[:, :, low:high], 0, 1).reshape(rows, -1).astype(F32)

    def with_gain(weight, grad):
        return gain * grad, jnp.sum(weight.astype(F32) * grad, axis=1)

    query = 2 * small.wide
    key, ab = query + small.narrow, query + 2 * small.narrow
    g_in = [joined(query, key), joined(key, ab), joined(small.wide, query)]
    g_in, norm_a = with_gain(mixer_in, jnp.concatenate(g_in, axis=1))
    g_gate, norm_b = with_gain(gate_weight, joined(0, small.wide))
    g_ab = jnp.concatenate([joined(ab, ab + heads), joined(ab + heads, ab + 2 * heads)], axis=1)
    g_ab, norm_c = with_gain(alpha_beta, g_ab)
    return norm_a + norm_b + norm_c, g_in, g_gate, g_ab


def masked(out_cotangent, slot_length, me):
    slots, seg, unused = out_cotangent.shape
    positions = me * seg + lax.broadcasted_iota(jnp.int32, (slots, seg), 1)
    return out_cotangent.astype(F32) * (positions < slot_length[:, None]).astype(F32)[..., None]


def feed_forward(pre, g_hidden):
    half = pre.shape[1] // 2
    u, w = pre[:, :half].astype(F32), pre[:, half:].astype(F32)
    sig = sigmoid(u)
    g_u = g_hidden * w * (sig * (1.0 + u * (1.0 - sig)))
    return (u * sig * w).astype(BF16), jnp.concatenate([g_u, g_hidden * (u * sig)], axis=1).astype(BF16)


def on_device(
    inputs, out_cotangent, slot_length, mixer_norm, mixer_in, gate_weight, alpha_beta, conv_taps,
    decay_log, decay_bias, head_norm, mixer_out, feed_norm, gate_up, down_weight,
):
    lines = Lines()
    run = on_known if lines.known else on_any
    return run(
        lines, Small(lines, conv_taps, head_norm),
        inputs, out_cotangent, slot_length, mixer_norm, mixer_in, gate_weight, alpha_beta, conv_taps,
        decay_log, decay_bias, head_norm, mixer_out, feed_norm, gate_up, down_weight,
    )


def on_any(
    lines, small,
    inputs, out_cotangent, slot_length, mixer_norm, mixer_in, gate_weight, alpha_beta, conv_taps,
    decay_log, decay_bias, head_norm, mixer_out, feed_norm, gate_up, down_weight,
):
    shards = lines.count
    slots, seg, width = inputs.shape
    rows, ff = mixer_in.shape[0], down_weight.shape[0]
    flat = lambda item: item.reshape((shards * slots * seg,) + item.shape[3:])
    unflat = lambda item: item.reshape((shards, slots, seg) + item.shape[1:])
    gather = lambda item: lax.all_gather(item, "shard", axis=0)
    scatter = lambda item: lax.psum_scatter(unflat(item.astype(BF16)), "shard", scatter_dimension=0, tiled=False).astype(F32)
    swap = lambda item: lax.all_to_all(item, "shard", 0, 0)
    gain_in, gain_feed = mixer_norm.astype(F32)[:, None], feed_norm.astype(F32)[:, None]
    scaled = lambda weight, gain: (weight.astype(F32) * gain).astype(BF16)
    taps, gain = small.parameters(gather(jnp.concatenate([conv_taps.reshape(-1), head_norm])).astype(F32))
    decay = small.decay(decay_log, decay_bias)
    w_mixer = swap(mixer_parts(scaled(mixer_in, gain_in), scaled(gate_weight, gain_in), scaled(alpha_beta, gain_in), shards))
    w_mixer = w_mixer.reshape(width, -1)
    up_rows = scaled(gate_up, gain_feed).reshape(rows, 2, shards, ff)
    w_up = swap(jnp.transpose(up_rows, (2, 0, 1, 3))).reshape(width, 2 * ff)
    x = inputs.astype(F32)
    x_rate = rms_rate(x)
    x_all = flat(gather((x * x_rate).astype(BF16)))
    comb = unflat(mm(x_all, w_mixer).astype(BF16))
    order = lax.iota(jnp.int32, shards)
    spans = shards * seg // SPAN
    held, unused = mix_forward(0, spans, [], None, order, comb, taps, decay, gain)
    g_out = masked(out_cotangent, slot_length, lines.me)
    g_out_all = flat(gather(g_out.astype(BF16)))
    resid = x + scatter(mm(flat(held[0]), mixer_out))
    rate = rms_rate(resid)
    feed_all = flat(gather((resid * rate).astype(BF16)))
    hidden, g_pre = feed_forward(mm(feed_all, w_up).astype(BF16), mm_nt(g_out_all, down_weight))
    layer_out = (resid + scatter(mm(hidden, down_weight))).astype(BF16)
    g_resid = g_out + rms_back(resid, rate, scatter(mm_nt(g_pre, w_up)))
    g_resid_all = flat(gather(g_resid.astype(BF16)))
    g_head = unflat(mm_nt(g_resid_all, mixer_out).astype(BF16))
    grads, terms, unused = mix_backward(0, spans, [], None, order, comb, taps, decay, gain, held[1:], g_head)
    g_mixer = flat(grads[0])
    input_grad = (g_resid + rms_back(x, x_rate, scatter(mm_nt(g_mixer, w_mixer)))).astype(BF16)
    total = lambda item: lax.psum(item.astype(BF16), "rep").astype(F32)
    owned = swap(total(mm_tn(x_all, g_mixer)).astype(BF16).reshape(shards, rows, -1))
    g_norm, g_in, g_gate, g_ab = mixer_grads(small, owned, mixer_norm, mixer_in, gate_weight, alpha_beta)
    up_owned = swap(total(mm_tn(feed_all, g_pre)).astype(BF16).reshape(shards, rows, 2, ff)).astype(F32)
    up_owned = jnp.transpose(up_owned, (1, 2, 0, 3)).reshape(rows, -1)
    g_feed_norm = jnp.sum(up_owned * gate_up.astype(F32), axis=1)
    g_taps, g_gain, g_log, g_bias = small.gradients(gather(lax.psum(small.terms(*terms), "rep")))
    return (
        layer_out, input_grad, g_norm, g_in, g_gate, g_ab, g_taps, g_log, g_bias, g_gain,
        total(mm_tn(flat(held[0]), g_resid_all)), g_feed_norm, gain_feed * up_owned, total(mm_tn(hidden, g_out_all)),
    )


def on_known(
    lines, small,
    inputs, out_cotangent, slot_length, mixer_norm, mixer_in, gate_weight, alpha_beta, conv_taps,
    decay_log, decay_bias, head_norm, mixer_out, feed_norm, gate_up, down_weight,
):
    far, near, copies = lines.far, lines.near, COPIES
    slots, seg, width = inputs.shape
    piece = slots * seg
    rows, ff = mixer_in.shape[0], down_weight.shape[0]
    chans, wide = small.chans, small.wide
    flat = lambda item: item.reshape((-1,) + item.shape[3:])
    unflat = lambda item: item.reshape((-1, slots, seg) + item.shape[1:])
    at = lambda item, *places: jnp.concatenate([item[p] for p in places]) if len(places) > 1 else item[places[0]]
    f = Flow()
    copy = lines.copy.astype(jnp.int32)[None]
    shape = (NEAR, slots, seg, width)

    def ring(item):
        got_1, over_0 = lines.out_1(item), lines.over(item)
        line_1 = lines.line_1(got_1)
        got_2, over_1 = lines.out_2(got_1), lines.over(line_1)
        line_2 = lines.line_2(got_1, got_2)
        got_3, over_2 = lines.out_3(got_2), lines.over(line_2)
        line_3 = lines.line_3(got_2, got_3)
        return item, over_0, line_1, over_1, line_2, over_2, line_3, lines.over(line_3)

    def plane(item):
        by_chip, by_near = lines.to_chip(item), lines.over(item)
        both = jnp.stack([lines.to_chip(by_near[0]), lines.over(by_chip[1])])
        cores = lines.to_core(jnp.stack([by_chip, by_near]))
        return item, lines.to_core(item), by_chip, cores[0], by_near, cores[1], both, lines.to_core(both)

    x = inputs.astype(F32)
    f.x_all = flat(jnp.stack(ring((x * rms_rate(x)).astype(BF16))))
    gain_in, gain_feed = mixer_norm.astype(F32)[:, None], feed_norm.astype(F32)[:, None]
    extra = as_extra(jnp.concatenate([conv_taps.reshape(-1), head_norm]), rows)
    quarter = lax.all_to_all(pack_mixer(copy, mixer_in, gate_weight, alpha_beta, gain_in, extra), "shard", 0, 0)
    by_chip = lines.to_chip(quarter)
    w_mixer = lines.quarters(quarter, lines.to_core(quarter), by_chip, lines.to_core(by_chip))
    f.w_mixer = jnp.moveaxis(w_mixer, 0, 1).reshape(width, -1)
    f.decay = small.decay(decay_log, decay_bias)
    f.order = lines.order()
    cut = ff // copies
    group = (2 * cut + 127) // 128 * 128
    half_ff = 2 * group
    sides = jnp.stack([near, 1 - near])[:, None]
    blocks = jnp.arange(2 * FAR)
    starts = blocks // FAR * (FAR * NEAR * ff) + ff * (NEAR * (blocks % FAR) + sides) + cut * lines.copy
    picked = pick_columns(gate_up, gain_feed, starts.astype(jnp.int32), cut, group)
    f.picked = [picked[0], picked[1]]
    f.g_low = masked(out_cotangent, slot_length, lines.me).astype(BF16)
    f.down = lines.own_quarter(down_weight)
    f.step()

    f.up_over = lines.over(f.picked[1])
    ab_at = 2 * wide + 2 * small.narrow
    extra = f.w_mixer[:, ab_at + EXTRA : ab_at + EXTRA + WIDTH].reshape(FAR * NEAR, rows * WIDTH).astype(F32)
    f.taps, f.gain = small.parameters(extra[:, : CONV * small.chan_part + small.gain_part])
    f.g_core = lines.to_core(f.g_low)
    f.comb = unflat(mm(f.x_all, f.w_mixer))
    f.step()

    own, other = f.take(f.picked)[0], f.take(f.up_over)
    f.up = jnp.where(near == 0, jnp.stack([own, other]), jnp.stack([other, own]))
    f.up_1 = lines.out_1(f.up)
    f.g_chip, f.g_near = lines.to_chip(f.g_low), lines.over(f.g_low)
    mixing = lambda: (f.order, f.comb, f.taps, f.decay, f.gain)
    f.held, f.links = mix_forward(0, 8, [], None, *mixing())
    f.step()

    f.up_2 = lines.out_2(f.up_1)
    f.g_both = [lines.to_chip(f.g_near[0]), lines.over(f.g_chip[1])]
    f.g_cores = lines.to_core(jnp.stack([f.g_chip, f.g_near]))
    f.held, f.links = mix_forward(8, 8, f.held, f.links, *mixing())
    f.step()

    to_out = lambda row: mm(flat(f.held[0][NEAR * row : NEAR * row + NEAR]), mixer_out).astype(BF16).reshape(shape)
    f.out_3 = to_out(3)
    f.step()

    up_3 = lines.out_3(f.up_2)
    f.got = lines.over(f.out_3[1])
    f.out_2, f.out_1, f.out_0 = to_out(2), to_out(1), to_out(0)
    f.g_both = jnp.stack(f.g_both)
    f.g_both_core = lines.to_core(f.g_both)
    f.step()

    f.sum_3 = low_sum(f.take(f.out_3)[0], f.take(f.got))
    f.got_3 = lines.in_3(f.sum_3)
    f.got = lines.over(f.out_2[1])
    g_cores = f.take(f.g_cores)
    f.g_all = jnp.stack([f.g_low, f.g_core, f.g_chip, g_cores[0], f.g_near, g_cores[1], *f.take(f.g_both, f.g_both_core)])
    f.g_all = flat(f.g_all)
    f.take(f.g_low, f.g_core, f.g_chip, f.g_near)
    f.up_3 = up_3
    f.step()

    f.sum_2 = low_sum(f.take(f.out_2)[0], f.take(f.got))
    f.got_2 = lines.in_2(f.take(f.sum_3), f.take(f.got_3), f.sum_2)
    f.got = lines.over(f.out_1[1])
    f.w_up = lines.line_whole(*f.take(f.up, f.up_1, f.up_2, f.up_3)).reshape(width, 2 * half_ff)
    f.step()

    sum_1 = low_sum(f.take(f.out_1)[0], f.take(f.got))
    f.got_1 = lines.in_1(f.take(f.sum_2), f.take(f.got_2), sum_1)
    f.got = lines.over(f.out_0[1])
    f.step()

    own = f.take(f.out_0)[0].astype(F32) + f.take(f.got).astype(F32)
    f.resid = resid = inputs.astype(F32) + lines.sum_0(own, f.take(f.got_1))
    f.feed = (resid * rms_rate(resid)).astype(BF16)
    f.step()

    f.feed_all = flat(jnp.stack(plane(f.take(f.feed))))
    down_1 = lines.out_1(f.down)
    down_2 = lines.out_2(down_1)
    w_down = lines.line_whole(f.take(f.down), down_1, down_2, lines.out_3(down_2)).reshape(2, 2 * cut, width)
    f.w_down = jnp.pad(w_down, ((0, 0), (0, group - 2 * cut), (0, 0))).reshape(half_ff, width)
    pre = mm(f.feed_all, f.w_up)
    f.hidden, f.g_pre = feed_forward(pre, mm_nt(f.g_all, f.w_down))
    f.step()

    by_piece = lambda item: item.reshape(-1, piece, item.shape[1])
    to_feed = lambda *places: unflat(
        mm_nt(at(by_piece(f.g_pre), *places).reshape(-1, 2 * half_ff), f.w_up).astype(BF16)
    )
    f.back_3 = to_feed(6, 7)
    f.step()

    f.core_3 = lines.to_core(f.back_3[1])
    f.back_12 = to_feed(2, 4, 3, 5)
    f.step()

    f.core_12 = lines.to_core(f.back_12[2:])
    sum_3 = low_sum(f.take(f.back_3)[0], f.take(f.core_3))
    f.half_chip, f.half_near = lines.to_chip(sum_3[0]), lines.over(sum_3[1])
    f.back_0 = to_feed(0, 1)
    f.step()

    back, got = f.take(f.back_12, f.core_12)
    half_chip, half_near = f.take(f.half_chip, f.half_near)
    by_chip, by_near = low_sum(back[0], got[0]), low_sum(back[1], got[1])
    f.b_near = lines.over(jnp.stack([low_sum(by_near[0], half_chip), by_near[1]]))
    f.b_chip = lines.to_chip(jnp.stack([by_chip[0], low_sum(by_chip[1], half_near)]))
    f.core_0 = lines.to_core(f.back_0[1])
    f.out_part = mm(f.hidden, f.w_down).astype(BF16).reshape(4, 2, slots, seg, width)
    f.step()

    g_feed = f.take(f.back_0)[0].astype(F32)
    for item in f.take(f.core_0, f.b_chip, f.b_near):
        g_feed = g_feed + item.astype(F32)
    g_out = masked(out_cotangent, slot_length, lines.me)
    f.g_resid = g_resid = g_out + rms_back(f.resid, rms_rate(f.resid), g_feed)
    f.r_low = g_resid.astype(BF16)
    f.step()

    f.r_1, f.over_0 = lines.out_1(f.r_low), lines.over(f.r_low)
    f.up_term = mm_tn(f.take(f.feed_all), f.take(f.g_pre)).astype(BF16).reshape(FAR, NEAR, rows, 2 * half_ff)
    f.step()

    f.line_1 = lines.line_1(f.r_1)
    f.r_2, f.over_1 = lines.out_2(f.r_1), lines.over(f.line_1)
    f.out_core = lines.to_core(f.out_part[:, 1])
    f.u_3 = taken(f.up_term, lines.rows[3])
    u_got_3 = lines.in_3(f.u_3)
    down_term = mm_tn(f.take(f.hidden), f.take(f.g_all)).reshape(2, group, width)[:, : 2 * cut]
    f.down_term = down_term.astype(BF16).reshape(FAR, cut, width)
    f.step()

    f.line_2 = lines.line_2(f.take(f.r_1), f.r_2)
    f.r_3, f.over_2 = lines.out_3(f.r_2), lines.over(f.line_2)
    f.out_sum = low_sum(f.take(f.out_part)[:, 0], f.take(f.out_core))
    f.u_got_3 = u_got_3
    f.d_3 = taken(f.down_term, lines.rows[3])
    d_got_3 = lines.in_3(f.d_3)
    f.step()

    line_3 = lines.line_3(f.take(f.r_2), f.take(f.r_3))
    over_3 = lines.over(line_3)
    early = f.take(f.r_low, f.over_0, f.line_1, f.over_1, f.line_2, f.over_2)
    to_head = lambda *items: unflat(mm_nt(flat(jnp.stack(items)), mixer_out))
    f.g_head = jnp.concatenate([to_head(*early), to_head(line_3, over_3)])
    f.r_all = flat(jnp.stack(early + [line_3, over_3]))
    f.half_chip = lines.to_chip(f.out_sum[3, 0])
    f.u_2 = taken(f.up_term, lines.rows[2])
    u_got_2 = lines.in_2(f.take(f.u_3), f.take(f.u_got_3), f.u_2)
    f.d_got_3 = d_got_3
    f.step()

    def backward(first, steps, held, links):
        held, terms, links = mix_backward(first, steps, held, links, *mixing(), f.held[1:], f.g_head)
        f.grads, f.back_links = held, links
        f.terms = [a + b for a, b in zip(f.terms, terms)] if first else terms

    f.d_2 = taken(f.down_term, lines.rows[2])
    f.d_got_2 = lines.in_2(f.take(f.d_3), f.take(f.d_got_3), f.d_2)
    f.half_near = lines.over(f.out_sum[3, 1])
    head_term = mm_tn(flat(f.held[0]), f.take(f.r_all)).astype(BF16).reshape(2, wide // 2, width)
    f.head_kept, f.head_given = taken(head_term, lines.core), taken(head_term, 1 - lines.core)
    backward(0, 8, [], None)
    f.u_got_2 = u_got_2
    f.step()

    f.u_got_1 = lines.in_1(f.take(f.u_2), f.take(f.u_got_2), taken(f.up_term, lines.rows[1]))
    out_sum, half_chip, half_near = f.take(f.out_sum, f.half_chip, f.half_near)
    f.own_out = out_sum[0]
    f.o_near = lines.over(jnp.stack([low_sum(out_sum[2, 0], half_chip), out_sum[2, 1]]))
    f.o_chip = lines.to_chip(jnp.stack([out_sum[1, 0], low_sum(out_sum[1, 1], half_near)]))
    f.head_half = low_sum(f.take(f.head_kept), lines.to_core(f.take(f.head_given)))
    head_chip = lines.to_chip(f.head_half)
    backward(8, 8, f.grads, f.back_links)
    f.step()

    f.g_mixer = f.take(f.grads)[0]
    term = mm_tn(f.x_all, flat(f.g_mixer)).astype(BF16)
    f.w_term = term.reshape(FAR * NEAR, 2, 2, rows // copies, -1)
    f.small = small.terms(*f.take(f.terms))
    f.small = f.small + lines.to_core(f.small)
    up_sum = lines.sum_0(taken(f.take(f.up_term), far), f.take(f.u_got_1)).astype(BF16)
    f.up_own, f.up_over = taken(up_sum, near), lines.over(taken(up_sum, 1 - near))
    f.d_got_1 = lines.in_1(*f.take(f.d_2, f.d_got_2), taken(f.down_term, lines.rows[1]))
    f.head_half = low_sum(f.head_half, head_chip)
    f.step()

    core_part = lambda which: lax.dynamic_index_in_dim(f.w_term, which, 2, keepdims=False)
    f.w_kept, f.w_got = core_part(lines.core), lines.to_core(core_part(1 - lines.core))
    f.take(f.w_term)
    to_norm = lambda row: mm_nt(flat(f.g_mixer[NEAR * row : NEAR * row + NEAR]), f.w_mixer).astype(BF16).reshape(shape)
    f.out_3 = to_norm(3)
    f.small = (f.small + lines.to_chip(f.small))[None]
    f.step()

    half = low_sum(*f.take(f.w_kept, f.w_got))
    chip_part = lambda which: lax.dynamic_index_in_dim(half, which, 1, keepdims=False)
    f.w_half, w_got = chip_part(lines.chip), lines.to_chip(chip_part(1 - lines.chip))
    f.got = lines.over(f.out_3[1])
    f.out_2 = to_norm(2)
    f.step()

    f.sum_3 = low_sum(f.take(f.out_3)[0], f.take(f.got))
    f.got_3 = lines.in_3(f.sum_3)
    f.got = lines.over(f.out_2[1])
    f.down_sum = lines.sum_0(taken(f.take(f.down_term), far), f.take(f.d_got_1)).astype(BF16)
    up_own, up_over = f.take(f.up_own, f.up_over)
    f.up_own = jnp.where(near == 0, jnp.stack([up_own, up_over]), jnp.stack([up_over, up_own]))
    f.w_got = w_got
    f.out_1, f.out_0 = to_norm(1), to_norm(0)
    f.step()

    w_own = lax.all_to_all(low_sum(*f.take(f.w_half, f.w_got)), "shard", 0, 0)
    f.sum_2 = low_sum(f.take(f.out_2)[0], f.take(f.got))
    f.got_2 = lines.in_2(f.take(f.sum_3), f.take(f.got_3), f.sum_2)
    f.got = lines.over(f.out_1[1])
    up_chip = lines.to_chip(f.up_own)
    f.head_core = lines.to_core(f.head_half)
    layer_out = f.resid
    for item in f.take(f.own_out, f.o_near, f.o_chip):
        layer_out = layer_out + item.astype(F32)
    f.layer_out = layer_out.astype(BF16)
    f.step()

    sum_1 = low_sum(f.take(f.out_1)[0], f.take(f.got))
    f.got_1 = lines.in_1(f.take(f.sum_2), f.take(f.got_2), sum_1)
    f.got = lines.over(f.out_0[1])
    f.down_core = lines.to_core(f.down_sum)
    ups = jnp.stack([f.up_own, lines.to_core(f.up_own), up_chip, lines.to_core(up_chip)])
    f.take(f.up_own)
    f.grad_up, f.up_dots = merge_columns(copy, ups, gate_up, gain_feed, cut, group)
    f.grad_out = spread(lines.core, f.take(f.head_half, f.head_core))
    f.down_chip = lines.to_chip(f.down_sum)
    f.w_own = w_own
    f.step()

    f.w_chip, f.w_core = lines.to_chip(f.w_own), lines.to_core(f.w_own)
    own = f.take(f.out_0)[0].astype(F32) + f.take(f.got).astype(F32)
    g_norm = lines.sum_0(own, f.take(f.got_1))
    xs = inputs.astype(F32)
    f.input_grad = (f.take(f.g_resid) + rms_back(xs, rms_rate(xs), g_norm)).astype(BF16)
    f.grad_down = spread(lines.copy, [f.down_sum, f.down_core, f.down_chip, lines.to_core(f.down_chip)])
    f.take(f.down_sum, f.down_core, f.down_chip)
    gathered = f.take(f.small)
    for bit in (1, 2, 4):
        gathered = jnp.concatenate([gathered, lines.crossed(gathered, bit)])
    gathered = jnp.take(gathered, lax.iota(jnp.int32, FAR * NEAR) ^ lines.me, axis=0)
    f.small_grads = small.gradients(gathered)
    f.step()

    quarters = [f.w_own, f.w_core, f.w_chip, lines.to_core(f.w_chip)]
    g_in, g_gate, dots_a = unpack_wide(copy, quarters, mixer_in, gate_weight, gain_in)
    g_in, g_ab, dots_b = unpack_narrow(copy, quarters, mixer_in, alpha_beta, gain_in, g_in)
    g_taps, g_gain, g_log, g_bias = f.small_grads
    return (
        f.layer_out, f.input_grad, dots_a[:, 0] + dots_b[:, 0], g_in, g_gate, g_ab, g_taps, g_log, g_bias, g_gain,
        f.grad_out, f.up_dots[:, 0], f.grad_up, f.grad_down,
    )


def solution(mesh):
    tokens, rows = P("rep", "shard", None), P("shard", None)
    return jax.shard_map(
        on_device,
        mesh=mesh,
        in_specs=(
            tokens, tokens, P("rep"), P("shard"), rows, rows, rows, P(None, "shard"), P(), P(),
            P("shard"), rows, P("shard"), rows, rows,
        ),
        out_specs=(
            tokens, tokens, P("shard"), rows, rows, rows, P(None, "shard"), P(), P(),
            P("shard"), rows, P("shard"), rows, rows,
        ),
        check_vma=False,
    )
```
